512 devices in a mesh: gx: 32 (over z_lo, y, core), gy: 16 (over x, z_hi).
Axes of the slice: x: 4, y: 4, z: 16 (z_hi: 4, z_lo: 4; z = z_hi * 4 + z_lo), core: 2. Of those that a mesh axis runs over, the one named last changes fastest.
Arguments:
- deflation: float32 [32, 320, 80, 128], P(None, 'gx', 'gy'), may hold values from -13 to 13
- layers: int32 [256, 48, 128], P('gx', 'gy'), may hold values from 0 to 84
- layer_table: float32 [85], replicated, may hold values from 0.02 to 2
- forcing: float32 [256, 48, 128], P('gx', 'gy'), may hold values from -13 to 13
Outputs:
- coarse_rows: float32 [32, 16, 9, 32, 32], P('gx', 'gy')
- coarse_solution: float32 [32, 16, 32], P('gx', 'gy')
The draws below stay inside these ranges and needn't reach their ends.
All inputs are finite; a program needn't handle non-finite values.
Results may differ from the reference program's by a relative error of at most 0.0003.
Values sent between devices are 32-bit elements; how exact they have to be, the bound alone decides.
A program may use at most 64 MiB of HBM per device.

```python
import math
import jax
import jax.numpy as jnp
from jax import lax

VEC = 32
CX = 8
CY = 3
CZ = 128
MARGIN = 1
LAYERS = 85
ITERS = 3
EX = 10
EY = 5
NX = 256
NY = 48
N_GX = 32
N_GY = 16


def draw_deflation(key, part):
    key_noise = jax.random.fold_in(key, 11)
    key_common = jax.random.fold_in(key, 12)
    length_x = NX // CX * EX
    length_y = NY // CY * EY
    offset_x = jnp.arange(length_x, dtype=jnp.int32)
    offset_y = jnp.arange(length_y, dtype=jnp.int32)
    index_x = jnp.clip(offset_x // EX * CX - MARGIN + offset_x % EX, 0, NX - 1)
    index_y = jnp.clip(offset_y // EY * CY - MARGIN + offset_y % EY, 0, NY - 1)
    noise = jnp.clip(jax.random.normal(key_noise, (VEC, length_x, length_y, CZ), jnp.float32), -4.0, 4.0)
    common = jnp.clip(jax.random.normal(key_common, (NX, NY, CZ), jnp.float32), -4.0, 4.0)
    shared = jnp.take(jnp.take(common, index_x, axis=0), index_y, axis=1)
    return (noise + shared[None]).astype(jnp.float32)


def draw_forcing(key, part):
    key_base = jax.random.fold_in(key, 21)
    place_x = jnp.arange(NX, dtype=jnp.float32) / NX
    rising = 1.0 + 2.0 * place_x
    base = jnp.clip(jax.random.normal(key_base, (NX, NY, CZ), jnp.float32), -4.0, 4.0)
    return (base * rising[:, None, None]).astype(jnp.float32)


def with_ends(drawn, rng, least, high):
    dims = drawn.shape
    place = [jax.random.randint(jax.random.fold_in(rng, axis), (), 0, dims[axis]) for axis in range(len(dims))]
    drawn = drawn.at[tuple(place)].set(least)
    longest = dims.index(max(dims))
    place[longest] = (place[longest] + 1) % dims[longest]
    return drawn.at[tuple(place)].set(high)


def setup_inputs(seed: int = 0) -> dict:
    arg_keys = jax.random.split(jax.random.key(seed), 5)
    return {
        "deflation": draw_deflation(jax.random.fold_in(arg_keys[4], 71), 0),
        "layers": with_ends(jax.random.randint(arg_keys[1], (NX, NY, CZ), 0, LAYERS), jax.random.fold_in(arg_keys[1], 1), 0, LAYERS - 1).astype(jnp.int32),
        "layer_table": jnp.clip(jnp.exp(jax.random.uniform(arg_keys[2], (LAYERS,), jnp.float32, math.log(0.02), math.log(2.0))), 0.02, 2.0),
        "forcing": draw_forcing(jax.random.fold_in(arg_keys[4], 71), 0),
    }


storage_term = 0.5

def unity_weights(index_pos, subdomains, own_cells):
    offset = jnp.arange(own_cells + 2 * MARGIN, dtype=jnp.int32)
    global_pos = index_pos * own_cells - MARGIN + offset
    inside = ((global_pos >= 0) & (global_pos < subdomains * own_cells)).astype(jnp.float32)
    below_side = ((index_pos > 0) & (global_pos < index_pos * own_cells + MARGIN)).astype(jnp.float32)
    above_side = ((index_pos < subdomains - 1) & (global_pos >= (index_pos + 1) * own_cells - MARGIN)).astype(jnp.float32)
    return inside / (1.0 + below_side + above_side)

def operate(padded, kappa_box):
    centre = padded[:, 1:-1, 1:-1]
    kappa_centre = kappa_box[1:-1, 1:-1]
    width_x = centre.shape[1]
    width_y = centre.shape[2]
    result = storage_term * centre
    for shift_x, shift_y in ((1, 0), (-1, 0), (0, 1), (0, -1)):
        beside = padded[:, 1 + shift_x:1 + shift_x + width_x, 1 + shift_y:1 + shift_y + width_y]
        kappa_beside = kappa_box[1 + shift_x:1 + shift_x + width_x, 1 + shift_y:1 + shift_y + width_y]
        result = result + jnp.sqrt(kappa_centre * kappa_beside) * (centre - beside)
    for forward in (True, False):
        if forward:
            beside = jnp.pad(centre[..., 1:], ((0, 0), (0, 0), (0, 0), (0, 1)))
            kappa_beside = jnp.pad(kappa_centre[..., 1:], ((0, 0), (0, 0), (0, 1)))
        else:
            beside = jnp.pad(centre[..., :-1], ((0, 0), (0, 0), (0, 0), (1, 0)))
            kappa_beside = jnp.pad(kappa_centre[..., :-1], ((0, 0), (0, 0), (1, 0)))
        result = result + jnp.sqrt(kappa_centre * kappa_beside) * (centre - beside)
    return result

def strip_bounds(shift, ext_cells):
    slab_depth = 2 * MARGIN + 1
    if shift < 0:
        return (ext_cells - slab_depth, 0, slab_depth)
    if shift == 0:
        return (0, 1, ext_cells)
    return (0, ext_cells + 2 - slab_depth, slab_depth)

def coarse_product(coarse_rows, vector):
    padded_vec = jnp.pad(vector, ((1, 1), (1, 1), (0, 0)))
    result = jnp.zeros_like(vector)
    for shift_x in (-1, 0, 1):
        for shift_y in (-1, 0, 1):
            slot_index = (shift_x + 1) * 3 + (shift_y + 1)
            moved = padded_vec[1 + shift_x:1 + shift_x + N_GX, 1 + shift_y:1 + shift_y + N_GY]
            result = result + jnp.einsum('xyvw,xyw->xyv', coarse_rows[:, :, slot_index], moved, precision=lax.Precision.HIGHEST)
    return result

def reference(deflation, layers, layer_table, forcing):
    permeability = layer_table[layers]
    kappa_pad = jnp.pad(permeability, ((MARGIN + 2, MARGIN + 2), (MARGIN + 2, MARGIN + 2), (0, 0)))
    forcing_pad = jnp.pad(forcing, ((MARGIN, MARGIN), (MARGIN, MARGIN), (0, 0)))
    basis_scale = 1.0 / math.sqrt(CX * CY * CZ)
    zero_index = jnp.int32(0)

    def basis_of(sub_x, sub_y):
        exists = ((sub_x >= 0) & (sub_x < N_GX) & (sub_y >= 0) & (sub_y < N_GY)).astype(jnp.float32)
        clip_x = jnp.clip(sub_x, 0, N_GX - 1).astype(jnp.int32)
        clip_y = jnp.clip(sub_y, 0, N_GY - 1).astype(jnp.int32)
        values = lax.dynamic_slice(deflation, (zero_index, (clip_x * EX).astype(jnp.int32), (clip_y * EY).astype(jnp.int32), zero_index), (VEC, EX, EY, CZ))
        weights = unity_weights(clip_x, N_GX, CX)[:, None, None] * unity_weights(clip_y, N_GY, CY)[None, :, None]
        return values * weights * (basis_scale * exists)

    def one_subdomain(flat_index):
        sub_x = (flat_index // N_GY).astype(jnp.int32)
        sub_y = (flat_index % N_GY).astype(jnp.int32)
        basis = basis_of(sub_x, sub_y)
        kappa_box = lax.dynamic_slice(kappa_pad, ((sub_x * CX).astype(jnp.int32), (sub_y * CY).astype(jnp.int32), zero_index), (EX + 4, EY + 4, CZ))
        forcing_ext = lax.dynamic_slice(forcing_pad, ((sub_x * CX).astype(jnp.int32), (sub_y * CY).astype(jnp.int32), zero_index), (EX, EY, CZ))
        applied = operate(jnp.pad(basis, ((0, 0), (2, 2), (2, 2), (0, 0))), kappa_box)
        coarse_load = jnp.dot(basis.reshape(VEC, -1), forcing_ext.reshape(-1), precision=lax.Precision.HIGHEST)
        blocks = []
        for shift_x in (-1, 0, 1):
            for shift_y in (-1, 0, 1):
                other = basis_of(sub_x + shift_x, sub_y + shift_y)
                start_nx, start_bx, length_x = strip_bounds(shift_x, EX)
                start_ny, start_by, length_y = strip_bounds(shift_y, EY)
                strip = other[:, start_nx:start_nx + length_x, start_ny:start_ny + length_y]
                region = applied[:, start_bx:start_bx + length_x, start_by:start_by + length_y]
                blocks.append(jnp.dot(region.reshape(VEC, -1), strip.reshape(VEC, -1).T, precision=lax.Precision.HIGHEST))
        return (jnp.stack(blocks), coarse_load)
    rows_flat, load_flat = lax.map(one_subdomain, jnp.arange(N_GX * N_GY, dtype=jnp.int32))
    coarse_rows = rows_flat.reshape(N_GX, N_GY, 9, VEC, VEC)
    coarse_load = load_flat.reshape(N_GX, N_GY, VEC)
    solution = jnp.zeros_like(coarse_load)
    residual = coarse_load
    direction = coarse_load
    norm_now = jnp.sum(residual * residual)
    for iteration in range(ITERS):
        mapped = coarse_product(coarse_rows, direction)
        step_size = norm_now / jnp.sum(direction * mapped)
        solution = solution + step_size * direction
        residual = residual - step_size * mapped
        norm_next = jnp.sum(residual * residual)
        direction = residual + norm_next / norm_now * direction
        norm_now = norm_next
    return (coarse_rows, solution)
```

```python
import functools
import math

import jax
import jax.numpy as jnp
from jax import lax
from jax.experimental import pallas as pl
from jax.experimental.pallas import tpu as pltpu
from jax.sharding import PartitionSpec as P

VEC = 32
CX = 8
CY = 3
CZ = 128
MARGIN = 1
LAYERS = 85
ITERS = 3
EX = 10
EY = 5
MESH = pl.DeviceIdType.MESH
F32 = jnp.float32
BF16 = jnp.bfloat16

EDGE = (0, 1, 2, 7, 8, 9)
DIRS = ((1, 0), (-1, 0), (0, 1), (0, -1), (1, 1), (-1, 1), (1, -1), (-1, -1))
SEND_X = {1: (8, 2), -1: (2, 2), 0: (2, 8)}
LAND_X = {1: (0, 2), -1: (10, 2), 0: (2, 8)}
SEND_Y = {1: (3, 2), -1: (2, 2), 0: (2, 3)}
LAND_Y = {1: (0, 2), -1: (5, 2), 0: (2, 3)}


def unity_weights(index_pos, subdomains, own_cells):
    offset = jnp.arange(own_cells + 2 * MARGIN, dtype=jnp.int32)
    global_pos = index_pos * own_cells - MARGIN + offset
    inside = ((global_pos >= 0) & (global_pos < subdomains * own_cells)).astype(F32)
    below_side = ((index_pos > 0) & (global_pos < index_pos * own_cells + MARGIN)).astype(F32)
    above_side = (
        (index_pos < subdomains - 1) & (global_pos >= (index_pos + 1) * own_cells - MARGIN)
    ).astype(F32)
    return inside / (1.0 + below_side + above_side)


def pack(cells):
    highs = [c.astype(BF16) for c in cells]
    lows = [(c - h.astype(F32)).astype(BF16) for c, h in zip(cells, highs)]
    high = jnp.concatenate(highs, axis=1)
    low = jnp.concatenate(lows, axis=1)
    return jnp.concatenate([high, low], axis=0)


def dot_cells(left, right):
    return lax.dot_general(
        pack(left), pack(right), (((1,), (1,)), ((), ())), preferred_element_type=F32
    )


def fold(wide):
    tall = wide[0:VEC] + wide[VEC:]
    return tall[:, 0:VEC] + tall[:, VEC:]


def squeeze_block(block):
    return jnp.concatenate([block[8 * g : 8 * g + 8] for g in range(4)], axis=1)


def spread_block(packed):
    return jnp.concatenate([packed[:, VEC * g : VEC * g + VEC] for g in range(4)], axis=0)


def kernel(
    nx, ny, basis, layers, table, forcing, rows, answer,
    field, weighted, image, strip_x, strip_y, strip_m, corner_r, corner_l,
    block_out, block_in, vec_out, vec_in, sum_out, sum_x, sum_y,
    f_send, f_recv, y_send, y_recv, s_send, s_recv, c_send, c_recv,
    b_send, b_recv, v_send, v_recv, a_send, a_recv,
):
    px = lax.axis_index("gx")
    py = lax.axis_index("gy")
    right, left = lax.rem(px + 1, nx), lax.rem(px + nx - 1, nx)
    upper, lower = lax.rem(py + 1, ny), lax.rem(py + ny - 1, ny)
    at_x = {1: right, -1: left, 0: px}
    at_y = {1: upper, -1: lower, 0: py}

    def remote(src, dst, send, recv, to):
        return pltpu.make_async_remote_copy(
            src_ref=src, dst_ref=dst, send_sem=send, recv_sem=recv, device_id=to, device_id_type=MESH
        )

    barrier = pltpu.get_barrier_semaphore()

    def greet_x(k, carry):
        pl.semaphore_signal(barrier, inc=1, device_id=(lax.rem(px + k, nx), py), device_id_type=MESH)
        return carry

    def greet_y(k, carry):
        pl.semaphore_signal(barrier, inc=1, device_id=(px, lax.rem(py + k, ny)), device_id_type=MESH)
        return carry

    lax.fori_loop(1, nx, greet_x, 0)
    lax.fori_loop(1, ny, greet_y, 0)
    for dx, dy in DIRS[4:]:
        pl.semaphore_signal(barrier, inc=1, device_id=(at_x[dx], at_y[dy]), device_id_type=MESH)

    entry = layers[...]

    def look_up(t, root):
        return jnp.where(entry == t, table[t], root)

    root = jnp.sqrt(lax.fori_loop(0, LAYERS, look_up, jnp.zeros((CX, CY, CZ), F32)))
    for x in range(CX):
        for y in range(CY):
            field[2 + x, 2 + y, 0:1, :] = root[x, y : y + 1, :]
            field[2 + x, 2 + y, 1:2, :] = forcing[x, y : y + 1, :]

    pl.semaphore_wait(barrier, nx + ny + 2)

    field_copies = []
    for n, (dx, dy) in enumerate(DIRS):
        sx, lx = SEND_X[dx]
        sy, ly = SEND_Y[dy]
        tx = LAND_X[dx][0]
        ty = LAND_Y[dy][0]
        field_copies.append(
            remote(
                field.at[pl.ds(sx, lx), pl.ds(sy, ly)],
                field.at[pl.ds(tx, lx), pl.ds(ty, ly)],
                f_send.at[n], f_recv.at[n], (at_x[dx], at_y[dy]),
            )
        )
        field_copies[-1].start()
    strip_copies = [
        remote(
            basis.at[ex, pl.ds(0, 3)], strip_y.at[n], y_send.at[n], y_recv.at[n], (px, lower)
        )
        for n, ex in enumerate(EDGE)
    ]
    for n in (0, 5, 1, 4, 2, 3):
        strip_copies[n].start()
    x_copy = remote(basis.at[pl.ds(0, 3)], strip_x, s_send.at[0], s_recv.at[0], (left, py))
    x_copy.start()

    empty = jnp.zeros((VEC, CZ), F32)
    for j in range(7):
        weighted[0, j] = empty
        weighted[11, j] = empty

    def zero_rows(i, carry):
        weighted[i, 0] = empty
        weighted[i, 6] = empty
        return carry

    lax.fori_loop(1, 11, zero_rows, 0)

    for copy in field_copies:
        copy.wait_recv()
    for copy in field_copies:
        copy.wait_send()

    @pl.when(px == 0)
    def _():
        field[0:2] = jnp.zeros((2, 7, 2, CZ), F32)

    @pl.when(px == nx - 1)
    def _():
        field[10:12] = jnp.zeros((2, 7, 2, CZ), F32)

    @pl.when(py == 0)
    def _():
        field[:, 0:2] = jnp.zeros((12, 2, 2, CZ), F32)

    @pl.when(py == ny - 1)
    def _():
        field[:, 5:7] = jnp.zeros((12, 2, 2, CZ), F32)

    lane1 = lax.broadcasted_iota(jnp.int32, (1, CZ), 1)
    lane32 = lax.broadcasted_iota(jnp.int32, (VEC, CZ), 1)

    def beside(value, lane):
        before = jnp.where(lane > 0, pltpu.roll(value, 1, 1), 0.0)
        after = jnp.where(lane < CZ - 1, pltpu.roll(value, CZ - 1, 1), 0.0)
        return before + after

    def scale(i, load):
        for j in range(1, 6):
            value = basis[i - 1, j - 1]
            weighted[i, j] = field[i, j, 0:1, :] * value
            load = load + field[i, j, 1:2, :] * value
        return load

    load = lax.fori_loop(1, 11, scale, empty)

    def image_inside(i, j):
        own = field[i, j, 0:1, :]
        near = (
            field[i - 1, j, 0:1, :] + field[i + 1, j, 0:1, :]
            + field[i, j - 1, 0:1, :] + field[i, j + 1, 0:1, :] + beside(own, lane1)
        )
        total = (
            weighted[i - 1, j] + weighted[i + 1, j] + weighted[i, j - 1] + weighted[i, j + 1]
            + beside(weighted[i, j], lane32)
        )
        image[i, j] = (0.5 + own * near) * basis[i - 1, j - 1] - own * total

    def image_above(i):
        image[i, 6] = -(field[i, 6, 0:1, :] * weighted[i, 5])

    def upper_rows(i, carry):
        image_inside(i, 4)
        image_inside(i, 5)
        image_above(i)
        return carry

    def lower_rows(i, carry):
        for j in (1, 2, 3):
            image_inside(i, j)
        return carry

    lax.fori_loop(4, 8, upper_rows, 0)
    m_copy = remote(
        image.at[pl.ds(4, 4), pl.ds(4, 3)], strip_m, s_send.at[1], s_recv.at[1], (px, upper)
    )
    m_copy.start()

    row_id = lax.broadcasted_iota(jnp.int32, (VEC, VEC), 0)
    col_id = lax.broadcasted_iota(jnp.int32, (VEC, VEC), 1)
    diagonal = row_id == col_id
    blank = jnp.zeros((1, CZ - VEC), F32)

    def as_row(column):
        return jnp.sum(jnp.where(diagonal, column, 0.0), axis=0, keepdims=True)

    def vec_copies(step):
        return [
            remote(
                vec_out.at[step], vec_in.at[step, n],
                v_send.at[step, n], v_recv.at[step, n], (at_x[dx], at_y[dy]),
            )
            for n, (dx, dy) in enumerate(DIRS)
        ]

    copies = [vec_copies(step) for step in range(ITERS)]

    def send_vector(step, value):
        vec_out[step] = jnp.concatenate([value, blank], axis=1)
        for copy in copies[step]:
            copy.start()

    load_row = as_row(jnp.sum(load, axis=1, keepdims=True))
    send_vector(0, load_row)

    lax.fori_loop(1, 4, upper_rows, 0)
    lax.fori_loop(8, 11, upper_rows, 0)
    lax.fori_loop(1, 11, lower_rows, 0)
    for j in (4, 5):
        image[0, j] = -(field[0, j, 0:1, :] * weighted[1, j])
    image[0, 6] = empty
    image[11, 6] = empty
    for j in range(1, 6):
        image[11, j] = -(field[11, j, 0:1, :] * weighted[10, j])

    def own_block(t, total):
        i = 1 + 2 * t
        cells = [(i + k, j) for k in (0, 1) for j in range(1, 6)]
        return total + dot_cells(
            [image[a, b] for a, b in cells], [basis[a - 1, b - 1] for a, b in cells]
        )

    rows[4] = fold(lax.fori_loop(0, 5, own_block, jnp.zeros((2 * VEC, 2 * VEC), F32)))

    def send_block(n, block, to):
        block_out[n] = squeeze_block(block)
        copy = remote(block_out.at[n], block_in.at[n], b_send.at[n], b_recv.at[n], to)
        copy.start()
        return copy

    x_copy.wait()
    block_x = fold(
        dot_cells(
            [image[9 + k, 1 + j] for k in range(3) for j in range(EY)],
            [strip_x[k, j] for k in range(3) for j in range(EY)],
        )
    )
    rows[7] = jnp.where(px < nx - 1, block_x, 0.0)
    block_copies = [send_block(0, block_x.T, (right, py))]

    corner_copies = {}
    for n in (0, 5, 1, 4, 2, 3):
        strip_copies[n].wait()
        if n < 3:
            copy = remote(strip_y.at[n], corner_r.at[n], c_send.at[n], c_recv.at[n], (left, py))
        else:
            copy = remote(strip_y.at[n], corner_l.at[n - 3], c_send.at[n], c_recv.at[n], (right, py))
        copy.start()
        corner_copies[n] = copy

    m_copy.wait()
    part_m = fold(
        dot_cells(
            [strip_m[k, j] for k in range(4) for j in range(3)],
            [basis[3 + k, j] for k in range(4) for j in range(3)],
        )
    )
    block_copies.append(send_block(1, part_m, (px, lower)))
    part_e = fold(
        dot_cells(
            [image[1 + k, 4 + j] for k in range(3) for j in range(3)],
            [strip_y[k, j] for k in range(3) for j in range(3)],
        )
        + dot_cells(
            [image[8 + k, 4 + j] for k in range(3) for j in range(3)],
            [strip_y[3 + k, j] for k in range(3) for j in range(3)],
        )
    )
    block_copies.append(send_block(2, part_e.T, (px, upper)))
    for n in range(3):
        corner_copies[n].wait()
    block_r = fold(
        dot_cells(
            [image[9 + k, 4 + j] for k in range(3) for j in range(3)],
            [corner_r[k, j] for k in range(3) for j in range(3)],
        )
    )
    block_copies.append(send_block(3, block_r.T, (right, upper)))
    for n in range(3, 6):
        corner_copies[n].wait()
    block_l = fold(
        dot_cells(
            [image[k, 4 + j] for k in range(3) for j in range(3)],
            [corner_l[k, j] for k in range(3) for j in range(3)],
        )
    )
    block_copies.append(send_block(4, block_l.T, (left, upper)))
    has_up, has_down = py < ny - 1, py > 0
    has_right, has_left = px < nx - 1, px > 0
    rows[8] = jnp.where(has_right & has_up, block_r, 0.0)
    rows[2] = jnp.where(has_left & has_up, block_l, 0.0)
    for copy in block_copies:
        copy.wait()
    rows[1] = jnp.where(has_left, spread_block(block_in[0]), 0.0)
    rows[5] = jnp.where(has_up, part_e + spread_block(block_in[1]), 0.0)
    rows[3] = jnp.where(has_down, part_m.T + spread_block(block_in[2]), 0.0)
    rows[0] = jnp.where(has_left & has_down, spread_block(block_in[3]), 0.0)
    rows[6] = jnp.where(has_right & has_down, spread_block(block_in[4]), 0.0)

    def product(step, own):
        for copy in copies[step]:
            copy.wait()
        total = rows[4] * own
        for n, (dx, dy) in enumerate(DIRS):
            total = total + rows[3 * (1 - dx) + 1 - dy] * vec_in[step, n][:, 0:VEC]
        return as_row(jnp.sum(total, axis=1, keepdims=True))

    def summed(step, values):
        value = jnp.concatenate(values + [jnp.zeros((1, CZ - len(values)), F32)], axis=1)
        for stage, count, inbox in ((0, nx, sum_x), (1, ny, sum_y)):
            sum_out[step, stage] = value
            send, recv = a_send.at[step, stage], a_recv.at[step, stage]

            def tell(k, carry, stage=stage, inbox=inbox, send=send, recv=recv):
                to = (lax.rem(px + k, nx), py) if stage == 0 else (px, lax.rem(py + k, ny))
                remote(sum_out.at[step, stage], inbox.at[step, k - 1], send, recv, to).start()
                return carry

            lax.fori_loop(1, count, tell, 0)
            remote(inbox.at[step], inbox.at[step], send, recv, (right, upper)).wait_recv()
            value = value + jnp.sum(inbox[step], axis=0)
        for stage, count, inbox in ((0, nx, sum_x), (1, ny, sum_y)):
            send, recv = a_send.at[step, stage], a_recv.at[step, stage]
            remote(inbox.at[step], inbox.at[step], send, recv, (right, upper)).wait_send()
        return [value[:, n : n + 1] for n in range(len(values))]

    def inner(a, b):
        return jnp.sum(a * b, axis=1, keepdims=True)

    residual = load_row
    direction = residual
    mapped = product(0, residual)
    norm, energy = summed(0, [inner(residual, residual), inner(residual, mapped)])
    step_size = norm / energy
    solution_row = step_size * direction
    for step in range(1, ITERS):
        residual = residual - step_size * mapped
        send_vector(step, residual)
        image_row = product(step, residual)
        norm_next, plain, cross = summed(
            step,
            [
                inner(residual, residual),
                inner(residual, image_row),
                inner(residual, mapped) + inner(direction, image_row),
            ],
        )
        ratio = norm_next / norm
        energy = plain + ratio * cross + ratio * ratio * energy
        direction = residual + ratio * direction
        mapped = image_row + ratio * mapped
        norm = norm_next
        step_size = norm / energy
        solution_row = solution_row + step_size * direction
    answer[0] = solution_row


def body(deflation, layers, layer_table, forcing):
    nx = lax.axis_size("gx")
    ny = lax.axis_size("gy")
    weights = (
        unity_weights(lax.axis_index("gx"), nx, CX)[:, None]
        * unity_weights(lax.axis_index("gy"), ny, CY)[None, :]
        * (1.0 / math.sqrt(CX * CY * CZ))
    )
    basis = jnp.transpose(deflation, (1, 2, 0, 3)) * weights[:, :, None, None]
    vmem = pl.BlockSpec(memory_space=pltpu.VMEM)
    dma = pltpu.SemaphoreType.DMA
    rows, answer = pl.pallas_call(
        functools.partial(kernel, nx, ny),
        out_shape=(
            jax.ShapeDtypeStruct((9, VEC, VEC), F32),
            jax.ShapeDtypeStruct((1, 1, VEC), F32),
        ),
        in_specs=[vmem, vmem, pl.BlockSpec(memory_space=pltpu.SMEM), vmem],
        out_specs=(vmem, vmem),
        scratch_shapes=[
            pltpu.VMEM((12, 7, 2, CZ), F32),
            pltpu.VMEM((12, 7, VEC, CZ), F32),
            pltpu.VMEM((12, 7, VEC, CZ), F32),
            pltpu.VMEM((3, EY, VEC, CZ), F32),
            pltpu.VMEM((6, 3, VEC, CZ), F32),
            pltpu.VMEM((4, 3, VEC, CZ), F32),
            pltpu.VMEM((3, 3, VEC, CZ), F32),
            pltpu.VMEM((3, 3, VEC, CZ), F32),
            pltpu.VMEM((5, 8, CZ), F32),
            pltpu.VMEM((5, 8, CZ), F32),
            pltpu.VMEM((ITERS, 1, CZ), F32),
            pltpu.VMEM((ITERS, 8, 1, CZ), F32),
            pltpu.VMEM((ITERS, 2, 1, CZ), F32),
            pltpu.VMEM((ITERS, nx - 1, 1, CZ), F32),
            pltpu.VMEM((ITERS, ny - 1, 1, CZ), F32),
            dma((8,)), dma((8,)), dma((6,)), dma((6,)), dma((2,)), dma((2,)),
            dma((6,)), dma((6,)), dma((5,)), dma((5,)),
            dma((ITERS, 8)), dma((ITERS, 8)), dma((ITERS, 2)), dma((ITERS, 2)),
        ],
        compiler_params=pltpu.CompilerParams(
            collective_id=0, has_side_effects=True, vmem_limit_bytes=32 * 1024 * 1024
        ),
        name="coarse",
    )(basis, layers, layer_table, forcing)
    return rows[None, None], answer


def solution(mesh):
    return jax.shard_map(
        body,
        mesh=mesh,
        in_specs=(P(None, "gx", "gy", None), P("gx", "gy", None), P(), P("gx", "gy", None)),
        out_specs=(P("gx", "gy", None, None, None), P("gx", "gy", None)),
        check_vma=False,
    )
```

```python
import functools
import math

import jax
import jax.numpy as jnp
from jax import lax
from jax.experimental import pallas as pl
from jax.experimental.pallas import tpu as pltpu
from jax.sharding import PartitionSpec as P

VEC = 32
CX = 8
CY = 3
CZ = 128
MARGIN = 1
LAYERS = 85
ITERS = 3
EX = 10
EY = 5
MESH = pl.DeviceIdType.MESH
F32 = jnp.float32
BF16 = jnp.bfloat16

EDGE = (0, 1, 2, 7, 8, 9)
DIRS = ((1, 0), (-1, 0), (0, 1), (0, -1), (1, 1), (-1, 1), (1, -1), (-1, -1))
SEND_X = {1: (8, 2), -1: (2, 2), 0: (2, 8)}
LAND_X = {1: (0, 2), -1: (10, 2), 0: (2, 8)}
SEND_Y = {1: (3, 2), -1: (2, 2), 0: (2, 3)}
LAND_Y = {1: (0, 2), -1: (5, 2), 0: (2, 3)}


HALO_X = {1: (7, 3, 0), -1: (0, 3, 9), 0: (0, 10, 1)}
HALO_Y = {1: (2, 3, 0), -1: (0, 3, 4), 0: (0, 5, 1)}
PAIRS = ((0, 0), (0, 1), (0, 2), (0, 3), (1, 1), (1, 2), (1, 3), (2, 2), (2, 3))
SHRINK = 0.125
QUIET = 1e-13


def sum_stages(nx, ny):
    low_x = 8 if nx % 8 == 0 else 2
    low_y = 4 if ny % 4 == 0 and ny > 4 else 2
    return (
        ((0, 1, low_x),),
        ((0, low_x, nx // low_x), (1, 1, low_y)),
        ((1, low_y, ny // low_y),),
    )


def members(digits):
    return math.prod(count for axis, stride, count in digits)


def two_sum(a, b):
    total = a + b
    back = total - a
    return total, (a - (total - back)) + (b - back)


def quick_sum(a, b):
    total = a + b
    return total, b - (total - a)


def halves(a):
    big = 4097.0 * a
    high = big - (big - a)
    return high, a - high


def two_product(a, b):
    product = a * b
    ah, al = halves(a)
    bh, bl = halves(b)
    return product, ((ah * bh - product) + ah * bl + al * bh) + al * bl


def add2(a, b):
    total, err = two_sum(a[0], b[0])
    return quick_sum(total, err + (a[1] + b[1]))


def mul2(a, b):
    product, err = two_product(a[0], b[0])
    return quick_sum(product, err + (a[0] * b[1] + a[1] * b[0]))


def neg2(a):
    return -a[0], -a[1]


def div2(a, b):
    first = a[0] / b[0]
    rest = add2(a, neg2(mul2(b, (first, jnp.zeros_like(first)))))
    return quick_sum(first, rest[0] / b[0])


def total2(terms):
    result = terms[0]
    for term in terms[1:]:
        result = add2(result, term)
    return result


def three_steps(gram):
    at = {}
    for (i, j), value in zip(PAIRS, gram):
        at[i, j] = at[j, i] = value
    one = (jnp.ones_like(gram[0][0]), jnp.zeros_like(gram[0][0]))
    residual, direction = [one], [one]
    solution = []
    norm = first = at[0, 0]
    for step in range(ITERS):
        size = len(direction)
        energy = total2(
            [
                mul2(mul2(direction[i], direction[j]), at[i, j + 1])
                for i in range(size)
                for j in range(size)
            ]
        )
        length = div2(norm, energy)
        if step > 0:
            live = norm[0] > QUIET * first[0]
            length = tuple(jnp.where(live, part, 0.0) for part in length)
        moved = [mul2(length, d) for d in direction]
        solution = [add2(x, m) for x, m in zip(solution, moved)] + moved[len(solution) :]
        if step == ITERS - 1:
            break
        back = [neg2(m) for m in moved]
        residual = [residual[0]] + [
            add2(residual[k], back[k - 1]) if k < len(residual) else back[k - 1]
            for k in range(1, size + 1)
        ]
        count = len(residual)
        terms = []
        for i in range(count):
            for j in range(i, count):
                term = mul2(mul2(residual[i], residual[j]), at[i, j])
                terms.append(term if i == j else (2.0 * term[0], 2.0 * term[1]))
        norm_next = total2(terms)
        ratio = div2(norm_next, norm)
        if step > 0:
            ratio = tuple(jnp.where(live, part, 0.0) for part in ratio)
        direction = [
            add2(residual[k], mul2(ratio, direction[k])) if k < size else residual[k]
            for k in range(count)
        ]
        norm = norm_next
    return [x[0] for x in solution]


def pack(cells):
    highs = [c.astype(BF16) for c in cells]
    lows = [(c - h.astype(F32)).astype(BF16) for c, h in zip(cells, highs)]
    high = jnp.concatenate(highs, axis=1)
    low = jnp.concatenate(lows, axis=1)
    return jnp.concatenate([high, low], axis=0)


def dot_cells(left, right):
    return lax.dot_general(
        pack(left), pack(right), (((1,), (1,)), ((), ())), preferred_element_type=F32
    )


def fold(wide):
    tall = wide[0:VEC] + wide[VEC:]
    return tall[:, 0:VEC] + tall[:, VEC:]


def squeeze_block(block):
    return jnp.concatenate([block[8 * g : 8 * g + 8] for g in range(4)], axis=1)


def spread_block(packed):
    return jnp.concatenate([packed[:, VEC * g : VEC * g + VEC] for g in range(4)], axis=0)


def kernel(
    nx, ny, raw_hbm, layers_hbm, table, forcing_hbm, rows, answer,
    basis, entry_in, force_in, field, weighted, image, diag, strip_x, strip_y, strip_m,
    corner_r, corner_l, block_out, block_in, spread_out, spread_in, whole, shaded, sum_out,
    l_sem, f_send, f_recv, y_send, y_recv, x_send, x_recv, m_send, m_recv, c_send, c_recv,
    b_send, b_recv, v_send, v_recv, a_send, a_recv, *sums,
):
    px = lax.axis_index("gx")
    py = lax.axis_index("gy")
    stages = sum_stages(nx, ny)
    loads = [
        pltpu.make_async_copy(src, dst, l_sem.at[n])
        for n, (src, dst) in enumerate(
            ((layers_hbm, entry_in), (forcing_hbm, force_in), (raw_hbm, basis))
        )
    ]
    for load_copy in loads:
        load_copy.start()
    right, left = lax.rem(px + 1, nx), lax.rem(px + nx - 1, nx)
    upper, lower = lax.rem(py + 1, ny), lax.rem(py + ny - 1, ny)
    at_x = {1: right, -1: left, 0: px}
    at_y = {1: upper, -1: lower, 0: py}
    has_right, has_left = px < nx - 1, px > 0
    has_up, has_down = py < ny - 1, py > 0

    def remote(src, dst, send, recv, to):
        return pltpu.make_async_remote_copy(
            src_ref=src, dst_ref=dst, send_sem=send, recv_sem=recv, device_id=to, device_id_type=MESH
        )

    barrier = pltpu.get_barrier_semaphore()

    def partner(digits, k):
        place = [px, py]
        for axis, stride, count in digits:
            step, k = k % count, k // count
            digit = lax.rem(lax.div(place[axis], stride), count)
            place[axis] = place[axis] + (lax.rem(digit + step, count) - digit) * stride
        return tuple(place)

    for dx, dy in DIRS:
        pl.semaphore_signal(barrier, inc=1, device_id=(at_x[dx], at_y[dy]), device_id_type=MESH)
    for digits in stages:
        for k in range(1, members(digits)):
            pl.semaphore_signal(barrier, inc=1, device_id=partner(digits, k), device_id_type=MESH)

    loads[0].wait()
    entry = entry_in[...]

    def look_up(t, root):
        for k in range(5):
            root = jnp.where(entry == 5 * t + k, table[5 * t + k], root)
        return root

    root = jnp.sqrt(lax.fori_loop(0, LAYERS // 5, look_up, jnp.zeros((CY, CX, CZ), F32)))
    loads[1].wait()
    for x in range(CX):
        for y in range(CY):
            field[2 + x, 2 + y, 0:1, :] = root[y, x : x + 1, :]
            field[2 + x, 2 + y, 1:2, :] = force_in[y, x : x + 1, :]

    def weights_of(cells, has_below, has_above):
        low, high = jnp.where(has_below, 0.5, 1.0), jnp.where(has_above, 0.5, 1.0)
        low_end, high_end = jnp.where(has_below, 0.5, 0.0), jnp.where(has_above, 0.5, 0.0)
        return [low_end, low] + [1.0] * (cells - 4) + [high, high_end]

    scale_x = [w * (1.0 / math.sqrt(CX * CY * CZ)) for w in weights_of(EX, has_left, has_right)]
    scale_y = weights_of(EY, has_down, has_up)
    loads[2].wait()
    for ex in range(EX):
        for ey in range(EY):
            basis[ex, ey] = basis[ex, ey] * (scale_x[ex] * scale_y[ey])

    pl.semaphore_wait(barrier, 8 + sum(members(d) - 1 for d in stages))

    field_copies = []
    for n, (dx, dy) in enumerate(DIRS):
        sx, lx = SEND_X[dx]
        sy, ly = SEND_Y[dy]
        tx = LAND_X[dx][0]
        ty = LAND_Y[dy][0]
        field_copies.append(
            remote(
                field.at[pl.ds(sx, lx), pl.ds(sy, ly)],
                field.at[pl.ds(tx, lx), pl.ds(ty, ly)],
                f_send.at[n], f_recv.at[n], (at_x[dx], at_y[dy]),
            )
        )
        field_copies[-1].start()
    strip_copies = [
        remote(
            basis.at[ex, pl.ds(0, 3)], strip_y.at[n], y_send.at[n], y_recv.at[n], (px, lower)
        )
        for n, ex in enumerate(EDGE)
    ]
    strip_copies[0].start()
    x_copy = remote(basis.at[pl.ds(0, 3)], strip_x, x_send, x_recv, (left, py))
    x_copy.start()

    empty = jnp.zeros((VEC, CZ), F32)
    for j in range(7):
        weighted[0, j] = empty
        weighted[11, j] = empty

    def zero_rows(i, carry):
        weighted[i, 0] = empty
        weighted[i, 6] = empty
        return carry

    lax.fori_loop(1, 11, zero_rows, 0)

    for copy in field_copies:
        copy.wait()

    @pl.when(px == 0)
    def _():
        field[0:2] = jnp.zeros((2, 7, 2, CZ), F32)

    @pl.when(px == nx - 1)
    def _():
        field[10:12] = jnp.zeros((2, 7, 2, CZ), F32)

    @pl.when(py == 0)
    def _():
        field[:, 0:2] = jnp.zeros((12, 2, 2, CZ), F32)

    @pl.when(py == ny - 1)
    def _():
        field[:, 5:7] = jnp.zeros((12, 2, 2, CZ), F32)

    lane1 = lax.broadcasted_iota(jnp.int32, (1, CZ), 1)
    lane32 = lax.broadcasted_iota(jnp.int32, (VEC, CZ), 1)

    def beside(value, lane):
        before = jnp.where(lane > 0, pltpu.roll(value, 1, 1), 0.0)
        after = jnp.where(lane < CZ - 1, pltpu.roll(value, CZ - 1, 1), 0.0)
        return before + after

    def scale(i, load):
        for j in range(1, 6):
            value = basis[i - 1, j - 1]
            own = field[i, j, 0:1, :]
            weighted[i, j] = own * value
            load = load + field[i, j, 1:2, :] * value
            near = (
                field[i - 1, j, 0:1, :] + field[i + 1, j, 0:1, :]
                + field[i, j - 1, 0:1, :] + field[i, j + 1, 0:1, :] + beside(own, lane1)
            )
            diag[i, j] = 0.5 + own * near
        return load

    load = lax.fori_loop(1, 11, scale, empty)

    row_id = lax.broadcasted_iota(jnp.int32, (VEC, VEC), 0)
    col_id = lax.broadcasted_iota(jnp.int32, (VEC, VEC), 1)
    diagonal = row_id == col_id

    def as_row(column):
        return jnp.sum(jnp.where(diagonal, column, 0.0), axis=0, keepdims=True)

    def halo_copies(step):
        result = []
        for n, (dx, dy) in enumerate(DIRS):
            sx, lx, unused = HALO_X[dx]
            sy, ly, unused = HALO_Y[dy]
            result.append(
                remote(
                    spread_out.at[step, pl.ds(sx, lx), pl.ds(sy, ly)],
                    spread_in.at[step, n, pl.ds(0, lx), pl.ds(0, ly)],
                    v_send.at[step, n], v_recv.at[step, n], (at_x[dx], at_y[dy]),
                )
            )
        return result

    halos = [halo_copies(step) for step in range(ITERS)]

    def send_spread(step, column):
        def spread(ex, carry):
            for ey in range(EY):
                spread_out[step, ex, ey] = jnp.sum(basis[ex, ey] * column, axis=0, keepdims=True)
            return carry

        lax.fori_loop(0, EX, spread, 0)
        for copy in halos[step]:
            copy.start()

    exists = {(1, 0): has_left, (-1, 0): has_right, (0, 1): has_down, (0, -1): has_up}

    def gather_back(step):
        whole[...] = jnp.zeros((12, 7, 1, CZ), F32)
        whole[1:11, 1:6] = spread_out[step]
        for n, (dx, dy) in enumerate(DIRS):
            halos[step][n].wait()
            lx, tx = HALO_X[dx][1:]
            ly, ty = HALO_Y[dy][1:]
            there = exists[dx, 0] if dy == 0 else exists[0, dy] if dx == 0 else exists[dx, 0] & exists[0, dy]
            piece = jnp.where(there, spread_in[step, n, 0:lx, 0:ly], 0.0)
            whole[tx : tx + lx, ty : ty + ly] = whole[tx : tx + lx, ty : ty + ly] + piece

        def shade(i, carry):
            for j in range(7):
                shaded[i, j] = field[i, j, 0:1, :] * whole[i, j]
            return carry

        lax.fori_loop(0, 12, shade, 0)

        def collect(i, total):
            for j in range(1, 6):
                near = (
                    shaded[i - 1, j] + shaded[i + 1, j] + shaded[i, j - 1] + shaded[i, j + 1]
                    + beside(shaded[i, j], lane1)
                )
                value = diag[i, j] * whole[i, j] - field[i, j, 0:1, :] * near
                total = total + basis[i - 1, j - 1] * value
            return total

        return jnp.sum(lax.fori_loop(1, 11, collect, empty), axis=1, keepdims=True) * SHRINK

    columns = [jnp.sum(load, axis=1, keepdims=True)]
    send_spread(0, columns[0])
    strip_copies[5].start()

    def image_inside(i, j):
        total = (
            weighted[i - 1, j] + weighted[i + 1, j] + weighted[i, j - 1] + weighted[i, j + 1]
            + beside(weighted[i, j], lane32)
        )
        image[i, j] = diag[i, j] * basis[i - 1, j - 1] - field[i, j, 0:1, :] * total

    def image_above(i):
        image[i, 6] = -(field[i, 6, 0:1, :] * weighted[i, 5])

    def upper_rows(i, carry):
        image_inside(i, 4)
        image_inside(i, 5)
        image_above(i)
        return carry

    def lower_rows(i, carry):
        for j in (1, 2, 3):
            image_inside(i, j)
        return carry

    lax.fori_loop(4, 8, upper_rows, 0)
    m_copies = [
        remote(image.at[4 + k, pl.ds(4, 3)], strip_m.at[k], m_send.at[k], m_recv.at[k], (px, upper))
        for k in range(4)
    ]
    m_copies[0].start()
    lax.fori_loop(1, 4, upper_rows, 0)
    lax.fori_loop(8, 11, upper_rows, 0)
    lax.fori_loop(1, 11, lower_rows, 0)
    for j in (4, 5):
        image[0, j] = -(field[0, j, 0:1, :] * weighted[1, j])
    image[0, 6] = empty
    image[11, 6] = empty
    for j in range(1, 6):
        image[11, j] = -(field[11, j, 0:1, :] * weighted[10, j])

    columns.append(gather_back(0))
    send_spread(1, columns[1])
    for copy in (strip_copies[1], m_copies[1], strip_copies[4], m_copies[2]):
        copy.start()

    def own_block(t, total):
        i = 1 + 2 * t
        cells = [(i + k, j) for k in (0, 1) for j in range(1, 6)]
        return total + dot_cells(
            [image[a, b] for a, b in cells], [basis[a - 1, b - 1] for a, b in cells]
        )

    rows[4] = fold(lax.fori_loop(0, 5, own_block, jnp.zeros((2 * VEC, 2 * VEC), F32)))

    def send_block(n, block, to):
        block_out[n] = squeeze_block(block)
        copy = remote(block_out.at[n], block_in.at[n], b_send.at[n], b_recv.at[n], to)
        copy.start()
        return copy

    columns.append(gather_back(1))
    send_spread(2, columns[2])
    for copy in (strip_copies[2], m_copies[3], strip_copies[3]):
        copy.start()

    x_copy.wait()
    block_x = fold(
        dot_cells(
            [image[9 + k, 1 + j] for k in range(3) for j in range(EY)],
            [strip_x[k, j] for k in range(3) for j in range(EY)],
        )
    )
    rows[7] = jnp.where(has_right, block_x, 0.0)
    block_copies = [send_block(0, block_x.T, (right, py))]

    corner_copies = {}

    def hand_on(n):
        strip_copies[n].wait()
        if n < 3:
            copy = remote(strip_y.at[n], corner_r.at[n], c_send.at[n], c_recv.at[n], (left, py))
        else:
            copy = remote(strip_y.at[n], corner_l.at[n - 3], c_send.at[n], c_recv.at[n], (right, py))
        copy.start()
        corner_copies[n] = copy

    hand_on(0)
    hand_on(5)
    columns.append(gather_back(2))

    blank = jnp.zeros((1, CZ - VEC), F32)
    vectors = [jnp.concatenate([as_row(c), blank], axis=1) for c in columns]
    slot = lax.broadcasted_iota(jnp.int32, (16, CZ), 0)
    lane16 = lax.broadcasted_iota(jnp.int32, (16, CZ), 1)
    one_side = other_side = jnp.zeros((16, CZ), F32)
    for n, (i, j) in enumerate(PAIRS):
        one_side = jnp.where(slot == n, vectors[i], one_side)
        other_side = jnp.where(slot == n, vectors[j], other_side)
    gram = two_product(one_side, other_side)
    for shift in (16, 8, 4, 2, 1):
        gram = add2(gram, tuple(pltpu.roll(part, CZ - shift, 1) for part in gram))
    value = tuple(
        jnp.sum(jnp.where(slot == lane16, part[:, 0:1], 0.0), axis=0, keepdims=True)
        for part in gram
    )

    sum_copies = []

    def tell(stage):
        sum_out[stage] = jnp.concatenate(value, axis=0)
        for k in range(1, members(stages[stage])):
            remote(
                sum_out.at[stage], sums[stage].at[k - 1],
                a_send.at[stage], a_recv.at[stage], partner(stages[stage], k),
            ).start()

    def hear(stage):
        whole_inbox = remote(
            sums[stage], sums[stage], a_send.at[stage], a_recv.at[stage], (right, upper)
        )
        whole_inbox.wait()
        result = value
        for k in range(1, members(stages[stage])):
            message = sums[stage][k - 1]
            result = add2(result, (message[0:1], message[1:2]))
        return result

    tell(0)
    hand_on(1)
    hand_on(4)
    value = hear(0)
    tell(1)
    for copy in m_copies:
        copy.wait()
    part_m = fold(
        dot_cells(
            [strip_m[k, j] for k in range(4) for j in range(3)],
            [basis[3 + k, j] for k in range(4) for j in range(3)],
        )
    )
    block_copies.append(send_block(1, part_m, (px, lower)))
    hand_on(2)
    hand_on(3)
    part_e = fold(
        dot_cells(
            [image[1 + k, 4 + j] for k in range(3) for j in range(3)],
            [strip_y[k, j] for k in range(3) for j in range(3)],
        )
        + dot_cells(
            [image[8 + k, 4 + j] for k in range(3) for j in range(3)],
            [strip_y[3 + k, j] for k in range(3) for j in range(3)],
        )
    )
    block_copies.append(send_block(2, part_e.T, (px, upper)))
    value = hear(1)
    tell(2)
    for n in range(3):
        corner_copies[n].wait()
    block_r = fold(
        dot_cells(
            [image[9 + k, 4 + j] for k in range(3) for j in range(3)],
            [corner_r[k, j] for k in range(3) for j in range(3)],
        )
    )
    block_copies.append(send_block(3, block_r.T, (right, upper)))
    for n in range(3, 6):
        corner_copies[n].wait()
    block_l = fold(
        dot_cells(
            [image[k, 4 + j] for k in range(3) for j in range(3)],
            [corner_l[k, j] for k in range(3) for j in range(3)],
        )
    )
    block_copies.append(send_block(4, block_l.T, (left, upper)))
    value = hear(2)
    steps = three_steps([tuple(part[:, n : n + 1] for part in value) for n in range(len(PAIRS))])
    found = SHRINK * (steps[0] * vectors[0] + steps[1] * vectors[1] + steps[2] * vectors[2])
    answer[0] = found[:, 0:VEC]

    rows[8] = jnp.where(has_right & has_up, block_r, 0.0)
    rows[2] = jnp.where(has_left & has_up, block_l, 0.0)
    for copy in block_copies:
        copy.wait()
    rows[1] = jnp.where(has_left, spread_block(block_in[0]), 0.0)
    rows[5] = jnp.where(has_up, part_e + spread_block(block_in[1]), 0.0)
    rows[3] = jnp.where(has_down, part_m.T + spread_block(block_in[2]), 0.0)
    rows[0] = jnp.where(has_left & has_down, spread_block(block_in[3]), 0.0)
    rows[6] = jnp.where(has_right & has_down, spread_block(block_in[4]), 0.0)


def body(deflation, layers, layer_table, forcing):
    nx = lax.axis_size("gx")
    ny = lax.axis_size("gy")
    vmem = pl.BlockSpec(memory_space=pltpu.VMEM)
    hbm = pl.BlockSpec(memory_space=pltpu.HBM)
    dma = pltpu.SemaphoreType.DMA
    stages = sum_stages(nx, ny)
    rows, answer = pl.pallas_call(
        functools.partial(kernel, nx, ny),
        out_shape=(
            jax.ShapeDtypeStruct((9, VEC, VEC), F32),
            jax.ShapeDtypeStruct((1, 1, VEC), F32),
        ),
        in_specs=[hbm, hbm, pl.BlockSpec(memory_space=pltpu.SMEM), hbm],
        out_specs=(vmem, vmem),
        scratch_shapes=[
            pltpu.VMEM((EX, EY, VEC, CZ), F32),
            pltpu.VMEM((CY, CX, CZ), jnp.int32),
            pltpu.VMEM((CY, CX, CZ), F32),
            pltpu.VMEM((12, 7, 2, CZ), F32),
            pltpu.VMEM((12, 7, VEC, CZ), F32),
            pltpu.VMEM((12, 7, VEC, CZ), F32),
            pltpu.VMEM((12, 7, 1, CZ), F32),
            pltpu.VMEM((3, EY, VEC, CZ), F32),
            pltpu.VMEM((6, 3, VEC, CZ), F32),
            pltpu.VMEM((4, 3, VEC, CZ), F32),
            pltpu.VMEM((3, 3, VEC, CZ), F32),
            pltpu.VMEM((3, 3, VEC, CZ), F32),
            pltpu.VMEM((5, 8, CZ), F32),
            pltpu.VMEM((5, 8, CZ), F32),
            pltpu.VMEM((ITERS, EX, EY, 1, CZ), F32),
            pltpu.VMEM((ITERS, 8, EX, EY, 1, CZ), F32),
            pltpu.VMEM((12, 7, 1, CZ), F32),
            pltpu.VMEM((12, 7, 1, CZ), F32),
            pltpu.VMEM((len(stages), 2, CZ), F32),
            dma((3,)), dma((8,)), dma((8,)), dma((6,)), dma((6,)), dma, dma,
            dma((4,)), dma((4,)), dma((6,)), dma((6,)), dma((5,)), dma((5,)),
            dma((ITERS, 8)), dma((ITERS, 8)), dma((len(stages),)), dma((len(stages),)),
            *[pltpu.VMEM((members(digits) - 1, 2, CZ), F32) for digits in stages],
        ],
        compiler_params=pltpu.CompilerParams(
            collective_id=0, has_side_effects=True, vmem_limit_bytes=32 * 1024 * 1024
        ),
        name="coarse",
    )(
        jnp.transpose(deflation, (1, 2, 0, 3)),
        jnp.transpose(layers, (1, 0, 2)),
        layer_table,
        jnp.transpose(forcing, (1, 0, 2)),
    )
    return rows[None, None], answer


def solution(mesh):
    return jax.shard_map(
        body,
        mesh=mesh,
        in_specs=(P(None, "gx", "gy", None), P("gx", "gy", None), P(), P("gx", "gy", None)),
        out_specs=(P("gx", "gy", None, None, None), P("gx", "gy", None)),
        check_vma=False,
    )
```

```python
import functools
import math

import jax
import jax.numpy as jnp
from jax import lax
from jax.experimental import pallas as pl
from jax.experimental.pallas import tpu as pltpu
from jax.sharding import PartitionSpec as P

VEC = 32
CX = 8
CY = 3
CZ = 128
MARGIN = 1
LAYERS = 85
ITERS = 3
EX = 10
EY = 5
MESH = pl.DeviceIdType.MESH
F32 = jnp.float32
BF16 = jnp.bfloat16

EDGE = (0, 1, 2, 7, 8, 9)
DIRS = ((0, 1), (0, -1), (1, 1), (-1, 1), (1, -1), (-1, -1), (1, 0), (-1, 0))
UP = tuple((n, r) for n in (0, 5, 1, 4) for r in range(3)) + ((2, 0), (2, 1), (3, 0), (3, 1))
DOWN = tuple((c, r) for c in (3, 4, 5, 6) for r in range(3)) + ((2, 2), (7, 2))
UP_SHARE = (0, 4, 4, 4, 4)
DOWN_SHARE = (0, 4, 3, 3, 4)
SEND_X = {1: (8, 2), -1: (2, 2), 0: (2, 8)}
LAND_X = {1: (0, 2), -1: (10, 2), 0: (2, 8)}
SEND_Y = {1: (3, 2), -1: (2, 2), 0: (2, 3)}
LAND_Y = {1: (0, 2), -1: (5, 2), 0: (2, 3)}


HALO_X = {1: (7, 3, 0), -1: (0, 3, 9), 0: (0, 10, 1)}
HALO_Y = {1: (2, 3, 0), -1: (0, 3, 4), 0: (0, 5, 1)}
PAIRS = ((0, 0), (0, 1), (0, 2), (0, 3), (1, 1), (1, 2), (1, 3), (2, 2), (2, 3))
SHRINK = 0.125
QUIET = 1e-13


def sum_stages(nx, ny):
    low_x = 8 if nx % 8 == 0 else 2
    low_y = 4 if ny % 4 == 0 and ny > 4 else 2
    return (
        ((0, 1, low_x),),
        ((0, low_x, nx // low_x), (1, 1, low_y)),
        ((1, low_y, ny // low_y),),
    )


def members(digits):
    return math.prod(count for axis, stride, count in digits)


def two_sum(a, b):
    total = a + b
    back = total - a
    return total, (a - (total - back)) + (b - back)


def quick_sum(a, b):
    total = a + b
    return total, b - (total - a)


def halves(a):
    big = 4097.0 * a
    high = big - (big - a)
    return high, a - high


def two_product(a, b):
    product = a * b
    ah, al = halves(a)
    bh, bl = halves(b)
    return product, ((ah * bh - product) + ah * bl + al * bh) + al * bl


def add2(a, b):
    total, err = two_sum(a[0], b[0])
    return quick_sum(total, err + (a[1] + b[1]))


def mul2(a, b):
    product, err = two_product(a[0], b[0])
    return quick_sum(product, err + (a[0] * b[1] + a[1] * b[0]))


def neg2(a):
    return -a[0], -a[1]


def div2(a, b):
    first = a[0] / b[0]
    rest = add2(a, neg2(mul2(b, (first, jnp.zeros_like(first)))))
    return quick_sum(first, rest[0] / b[0])


def total2(terms):
    result = terms[0]
    for term in terms[1:]:
        result = add2(result, term)
    return result


def three_steps(gram):
    at = {}
    for (i, j), value in zip(PAIRS, gram):
        at[i, j] = at[j, i] = value
    one = (jnp.ones_like(gram[0][0]), jnp.zeros_like(gram[0][0]))
    residual, direction = [one], [one]
    solution = []
    norm = first = at[0, 0]
    for step in range(ITERS):
        size = len(direction)
        energy = total2(
            [
                mul2(mul2(direction[i], direction[j]), at[i, j + 1])
                for i in range(size)
                for j in range(size)
            ]
        )
        length = div2(norm, energy)
        if step > 0:
            live = norm[0] > QUIET * first[0]
            length = tuple(jnp.where(live, part, 0.0) for part in length)
        moved = [mul2(length, d) for d in direction]
        solution = [add2(x, m) for x, m in zip(solution, moved)] + moved[len(solution) :]
        if step == ITERS - 1:
            break
        back = [neg2(m) for m in moved]
        residual = [residual[0]] + [
            add2(residual[k], back[k - 1]) if k < len(residual) else back[k - 1]
            for k in range(1, size + 1)
        ]
        count = len(residual)
        terms = []
        for i in range(count):
            for j in range(i, count):
                term = mul2(mul2(residual[i], residual[j]), at[i, j])
                terms.append(term if i == j else (2.0 * term[0], 2.0 * term[1]))
        norm_next = total2(terms)
        ratio = div2(norm_next, norm)
        if step > 0:
            ratio = tuple(jnp.where(live, part, 0.0) for part in ratio)
        direction = [
            add2(residual[k], mul2(ratio, direction[k])) if k < size else residual[k]
            for k in range(count)
        ]
        norm = norm_next
    return [x[0] for x in solution]


def pack(cells):
    highs = [c.astype(BF16) for c in cells]
    lows = [(c - h.astype(F32)).astype(BF16) for c, h in zip(cells, highs)]
    high = jnp.concatenate(highs, axis=1)
    low = jnp.concatenate(lows, axis=1)
    return jnp.concatenate([high, low], axis=0)


def dot_cells(left, right):
    return lax.dot_general(
        pack(left), pack(right), (((1,), (1,)), ((), ())), preferred_element_type=F32
    )


def fold(wide):
    tall = wide[0:VEC] + wide[VEC:]
    return tall[:, 0:VEC] + tall[:, VEC:]


def squeeze_block(block):
    return jnp.concatenate([block[8 * g : 8 * g + 8] for g in range(4)], axis=1)


def spread_block(packed):
    return jnp.concatenate([packed[:, VEC * g : VEC * g + VEC] for g in range(4)], axis=0)


def kernel(
    nx, ny, raw_hbm, layers_hbm, table, forcing_hbm, rows, answer,
    basis, entry_in, force_in, field, weighted, image, diag, strip_x, strip_y, strip_m,
    corner_r, corner_l, block_out, block_in, spread_out, spread_in, whole, shaded, sum_out,
    l_sem, f_send, f_recv, y_send, y_recv, x_send, x_recv, m_send, m_recv, c_send, c_recv,
    b_send, b_recv, v_send, v_recv, a_send, a_recv, *sums,
):
    px = lax.axis_index("gx")
    py = lax.axis_index("gy")
    stages = sum_stages(nx, ny)
    loads = [
        pltpu.make_async_copy(src, dst, l_sem.at[n])
        for n, (src, dst) in enumerate(
            ((layers_hbm, entry_in), (forcing_hbm, force_in), (raw_hbm, basis))
        )
    ]
    for load_copy in loads:
        load_copy.start()
    right, left = lax.rem(px + 1, nx), lax.rem(px + nx - 1, nx)
    upper, lower = lax.rem(py + 1, ny), lax.rem(py + ny - 1, ny)
    at_x = {1: right, -1: left, 0: px}
    at_y = {1: upper, -1: lower, 0: py}
    has_right, has_left = px < nx - 1, px > 0
    has_up, has_down = py < ny - 1, py > 0

    def remote(src, dst, send, recv, to):
        return pltpu.make_async_remote_copy(
            src_ref=src, dst_ref=dst, send_sem=send, recv_sem=recv, device_id=to, device_id_type=MESH
        )

    barrier = pltpu.get_barrier_semaphore()

    def partner(digits, k):
        place = [px, py]
        for axis, stride, count in digits:
            step, k = k % count, k // count
            digit = lax.rem(lax.div(place[axis], stride), count)
            place[axis] = place[axis] + (lax.rem(digit + step, count) - digit) * stride
        return tuple(place)

    for dx, dy in DIRS:
        pl.semaphore_signal(barrier, inc=1, device_id=(at_x[dx], at_y[dy]), device_id_type=MESH)
    for digits in stages:
        for k in range(1, members(digits)):
            pl.semaphore_signal(barrier, inc=1, device_id=partner(digits, k), device_id_type=MESH)

    loads[0].wait()
    entry = entry_in[...]

    def look_up(t, root):
        for k in range(5):
            root = jnp.where(entry == 5 * t + k, table[5 * t + k], root)
        return root

    root = jnp.sqrt(lax.fori_loop(0, LAYERS // 5, look_up, jnp.zeros((CY, CX, CZ), F32)))
    loads[1].wait()
    for x in range(CX):
        for y in range(CY):
            field[2 + x, 2 + y, 0:1, :] = root[y, x : x + 1, :]
            field[2 + x, 2 + y, 1:2, :] = force_in[y, x : x + 1, :]

    def weights_of(cells, has_below, has_above):
        low, high = jnp.where(has_below, 0.5, 1.0), jnp.where(has_above, 0.5, 1.0)
        low_end, high_end = jnp.where(has_below, 0.5, 0.0), jnp.where(has_above, 0.5, 0.0)
        return [low_end, low] + [1.0] * (cells - 4) + [high, high_end]

    scale_x = [w * (1.0 / math.sqrt(CX * CY * CZ)) for w in weights_of(EX, has_left, has_right)]
    scale_y = weights_of(EY, has_down, has_up)
    loads[2].wait()
    for ex in range(EX):
        for ey in range(EY):
            basis[ex, ey] = basis[ex, ey] * (scale_x[ex] * scale_y[ey])

    pl.semaphore_wait(barrier, 8 + sum(members(d) - 1 for d in stages))

    field_copies = []
    for n, (dx, dy) in enumerate(DIRS):
        sx, lx = SEND_X[dx]
        sy, ly = SEND_Y[dy]
        tx = LAND_X[dx][0]
        ty = LAND_Y[dy][0]
        field_copies.append(
            remote(
                field.at[pl.ds(sx, lx), pl.ds(sy, ly)],
                field.at[pl.ds(tx, lx), pl.ds(ty, ly)],
                f_send.at[n], f_recv.at[n], (at_x[dx], at_y[dy]),
            )
        )
        field_copies[-1].start()
    up_copies = [
        remote(basis.at[EDGE[n], r], strip_y.at[n, r], y_send.at[t], y_recv.at[t], (px, lower))
        for t, (n, r) in enumerate(UP)
    ]
    down_copies = [
        remote(image.at[c + 1, 4 + r], strip_m.at[t], m_send.at[t], m_recv.at[t], (px, upper))
        for t, (c, r) in enumerate(DOWN)
    ]

    def feed(gap):
        ups = up_copies[sum(UP_SHARE[:gap]) : sum(UP_SHARE[: gap + 1])]
        downs = down_copies[sum(DOWN_SHARE[:gap]) : sum(DOWN_SHARE[: gap + 1])]
        for t in range(max(len(ups), len(downs))):
            for copies in (ups, downs):
                if t < len(copies):
                    copies[t].start()

    feed(0)
    x_copy = remote(basis.at[pl.ds(0, 3)], strip_x, x_send, x_recv, (left, py))
    x_copy.start()

    empty = jnp.zeros((VEC, CZ), F32)
    for j in range(7):
        weighted[0, j] = empty
        weighted[11, j] = empty

    def zero_rows(i, carry):
        weighted[i, 0] = empty
        weighted[i, 6] = empty
        return carry

    lax.fori_loop(1, 11, zero_rows, 0)

    for copy in field_copies:
        copy.wait()

    @pl.when(px == 0)
    def _():
        field[0:2] = jnp.zeros((2, 7, 2, CZ), F32)

    @pl.when(px == nx - 1)
    def _():
        field[10:12] = jnp.zeros((2, 7, 2, CZ), F32)

    @pl.when(py == 0)
    def _():
        field[:, 0:2] = jnp.zeros((12, 2, 2, CZ), F32)

    @pl.when(py == ny - 1)
    def _():
        field[:, 5:7] = jnp.zeros((12, 2, 2, CZ), F32)

    lane1 = lax.broadcasted_iota(jnp.int32, (1, CZ), 1)
    lane32 = lax.broadcasted_iota(jnp.int32, (VEC, CZ), 1)

    def beside(value, lane):
        before = jnp.where(lane > 0, pltpu.roll(value, 1, 1), 0.0)
        after = jnp.where(lane < CZ - 1, pltpu.roll(value, CZ - 1, 1), 0.0)
        return before + after

    def scale(i, load):
        for j in range(1, 6):
            value = basis[i - 1, j - 1]
            own = field[i, j, 0:1, :]
            weighted[i, j] = own * value
            load = load + field[i, j, 1:2, :] * value
            near = (
                field[i - 1, j, 0:1, :] + field[i + 1, j, 0:1, :]
                + field[i, j - 1, 0:1, :] + field[i, j + 1, 0:1, :] + beside(own, lane1)
            )
            diag[i, j] = 0.5 + own * near
        return load

    load = lax.fori_loop(1, 11, scale, empty, unroll=5)

    row_id = lax.broadcasted_iota(jnp.int32, (VEC, VEC), 0)
    col_id = lax.broadcasted_iota(jnp.int32, (VEC, VEC), 1)
    diagonal = row_id == col_id

    def as_row(column):
        return jnp.sum(jnp.where(diagonal, column, 0.0), axis=0, keepdims=True)

    def halo_copies(step):
        result = []
        for n, (dx, dy) in enumerate(DIRS):
            sx, lx, unused = HALO_X[dx]
            sy, ly, unused = HALO_Y[dy]
            result.append(
                remote(
                    spread_out.at[step, pl.ds(sx, lx), pl.ds(sy, ly)],
                    spread_in.at[step, n, pl.ds(0, lx), pl.ds(0, ly)],
                    v_send.at[step, n], v_recv.at[step, n], (at_x[dx], at_y[dy]),
                )
            )
        return result

    halos = [halo_copies(step) for step in range(ITERS)]

    def send_spread(step, column):
        def spread(ex, carry):
            for ey in range(EY):
                spread_out[step, ex, ey] = jnp.sum(basis[ex, ey] * column, axis=0, keepdims=True)
            return carry

        lax.fori_loop(0, EX, spread, 0, unroll=True)
        for copy in halos[step]:
            copy.start()

    exists = {(1, 0): has_left, (-1, 0): has_right, (0, 1): has_down, (0, -1): has_up}

    def gather_back(step):
        whole[...] = jnp.zeros((12, 7, 1, CZ), F32)
        whole[1:11, 1:6] = spread_out[step]
        for n, (dx, dy) in enumerate(DIRS):
            halos[step][n].wait()
            lx, tx = HALO_X[dx][1:]
            ly, ty = HALO_Y[dy][1:]
            there = exists[dx, 0] if dy == 0 else exists[0, dy] if dx == 0 else exists[dx, 0] & exists[0, dy]
            piece = jnp.where(there, spread_in[step, n, 0:lx, 0:ly], 0.0)
            whole[tx : tx + lx, ty : ty + ly] = whole[tx : tx + lx, ty : ty + ly] + piece

        def shade(i, carry):
            for j in range(7):
                shaded[i, j] = field[i, j, 0:1, :] * whole[i, j]
            return carry

        lax.fori_loop(0, 12, shade, 0, unroll=True)

        def collect(i, total):
            for j in range(1, 6):
                near = (
                    shaded[i - 1, j] + shaded[i + 1, j] + shaded[i, j - 1] + shaded[i, j + 1]
                    + beside(shaded[i, j], lane1)
                )
                value = diag[i, j] * whole[i, j] - field[i, j, 0:1, :] * near
                total = total + basis[i - 1, j - 1] * value
            return total

        return jnp.sum(lax.fori_loop(1, 11, collect, empty, unroll=True), axis=1, keepdims=True) * SHRINK

    columns = [jnp.sum(load, axis=1, keepdims=True)]
    send_spread(0, columns[0])

    def image_inside(i, j):
        total = (
            weighted[i - 1, j] + weighted[i + 1, j] + weighted[i, j - 1] + weighted[i, j + 1]
            + beside(weighted[i, j], lane32)
        )
        image[i, j] = diag[i, j] * basis[i - 1, j - 1] - field[i, j, 0:1, :] * total

    def image_above(i):
        image[i, 6] = -(field[i, 6, 0:1, :] * weighted[i, 5])

    def upper_rows(i, carry):
        image_inside(i, 4)
        image_inside(i, 5)
        image_above(i)
        return carry

    def lower_rows(i, carry):
        for j in (1, 2, 3):
            image_inside(i, j)
        return carry

    lax.fori_loop(4, 8, upper_rows, 0)
    lax.fori_loop(1, 4, upper_rows, 0)
    lax.fori_loop(8, 11, upper_rows, 0)
    lax.fori_loop(1, 11, lower_rows, 0)
    for j in (4, 5):
        image[0, j] = -(field[0, j, 0:1, :] * weighted[1, j])
    for j in range(1, 6):
        image[11, j] = -(field[11, j, 0:1, :] * weighted[10, j])
    feed(1)

    columns.append(gather_back(0))
    send_spread(1, columns[1])

    def own_block(t, total):
        i = 1 + 2 * t
        cells = [(i + k, j) for k in (0, 1) for j in range(1, 6)]
        return total + dot_cells(
            [image[a, b] for a, b in cells], [basis[a - 1, b - 1] for a, b in cells]
        )

    rows[4] = fold(lax.fori_loop(0, 5, own_block, jnp.zeros((2 * VEC, 2 * VEC), F32)))
    feed(2)

    def send_block(n, block, to):
        block_out[n] = squeeze_block(block)
        copy = remote(block_out.at[n], block_in.at[n], b_send.at[n], b_recv.at[n], to)
        copy.start()
        return copy

    columns.append(gather_back(1))
    send_spread(2, columns[2])

    x_copy.wait()
    block_x = fold(
        dot_cells(
            [image[9 + k, 1 + j] for k in range(3) for j in range(EY)],
            [strip_x[k, j] for k in range(3) for j in range(EY)],
        )
    )
    rows[7] = jnp.where(has_right, block_x, 0.0)
    block_copies = [send_block(0, block_x.T, (right, py))]
    feed(3)

    corner_copies = {}

    def hand_on(n):
        for t in range(len(UP)):
            if UP[t][0] == n:
                up_copies[t].wait()
        part = pl.ds(0, 2 if n in (2, 3) else 3)
        inbox, to = (corner_r.at[n], left) if n < 3 else (corner_l.at[n - 3], right)
        copy = remote(strip_y.at[n, part], inbox.at[part], c_send.at[n], c_recv.at[n], (to, py))
        copy.start()
        corner_copies[n] = copy

    hand_on(0)
    hand_on(5)
    columns.append(gather_back(2))

    blank = jnp.zeros((1, CZ - VEC), F32)
    vectors = [jnp.concatenate([as_row(c), blank], axis=1) for c in columns]
    slot = lax.broadcasted_iota(jnp.int32, (16, CZ), 0)
    lane16 = lax.broadcasted_iota(jnp.int32, (16, CZ), 1)
    one_side = other_side = jnp.zeros((16, CZ), F32)
    for n, (i, j) in enumerate(PAIRS):
        one_side = jnp.where(slot == n, vectors[i], one_side)
        other_side = jnp.where(slot == n, vectors[j], other_side)
    gram = two_product(one_side, other_side)
    for shift in (16, 8, 4, 2, 1):
        gram = add2(gram, tuple(pltpu.roll(part, CZ - shift, 1) for part in gram))
    value = tuple(
        jnp.sum(jnp.where(slot == lane16, part[:, 0:1], 0.0), axis=0, keepdims=True)
        for part in gram
    )

    sum_copies = []

    def tell(stage):
        sum_out[stage] = jnp.concatenate(value, axis=0)
        for k in range(1, members(stages[stage])):
            remote(
                sum_out.at[stage], sums[stage].at[k - 1],
                a_send.at[stage], a_recv.at[stage], partner(stages[stage], k),
            ).start()

    def hear(stage):
        whole_inbox = remote(
            sums[stage], sums[stage], a_send.at[stage], a_recv.at[stage], (right, upper)
        )
        whole_inbox.wait()
        result = value
        for k in range(1, members(stages[stage])):
            message = sums[stage][k - 1]
            result = add2(result, (message[0:1], message[1:2]))
        return result

    tell(0)
    feed(4)
    hand_on(1)
    hand_on(4)
    value = hear(0)
    tell(1)
    for copy in down_copies:
        copy.wait()
    part_m = fold(
        dot_cells([strip_m[t] for t in range(len(DOWN))], [basis[c, r] for c, r in DOWN])
    )
    block_copies.append(send_block(1, part_m, (px, lower)))
    hand_on(2)
    hand_on(3)
    part_e = fold(
        dot_cells(
            [image[EDGE[n] + 1, 4 + r] for n, r in UP], [strip_y[n, r] for n, r in UP]
        )
    )
    block_copies.append(send_block(2, part_e.T, (px, upper)))
    for n in range(3):
        corner_copies[n].wait()
    block_r = fold(
        dot_cells(
            [image[9 + n, 4 + r] for n, r in UP if n < 3],
            [corner_r[n, r] for n, r in UP if n < 3],
        )
    )
    block_copies.append(send_block(3, block_r.T, (right, upper)))
    for n in range(3, 6):
        corner_copies[n].wait()
    block_l = fold(
        dot_cells(
            [image[n - 3, 4 + r] for n, r in UP if n > 2],
            [corner_l[n - 3, r] for n, r in UP if n > 2],
        )
    )
    block_copies.append(send_block(4, block_l.T, (left, upper)))
    value = hear(1)
    tell(2)
    value = hear(2)
    steps = three_steps([tuple(part[:, n : n + 1] for part in value) for n in range(len(PAIRS))])
    found = SHRINK * (steps[0] * vectors[0] + steps[1] * vectors[1] + steps[2] * vectors[2])
    answer[0] = found[:, 0:VEC]

    rows[8] = jnp.where(has_right & has_up, block_r, 0.0)
    rows[2] = jnp.where(has_left & has_up, block_l, 0.0)
    for copy in block_copies:
        copy.wait()
    rows[1] = jnp.where(has_left, spread_block(block_in[0]), 0.0)
    rows[5] = jnp.where(has_up, part_e + spread_block(block_in[1]), 0.0)
    rows[3] = jnp.where(has_down, part_m.T + spread_block(block_in[2]), 0.0)
    rows[0] = jnp.where(has_left & has_down, spread_block(block_in[3]), 0.0)
    rows[6] = jnp.where(has_right & has_down, spread_block(block_in[4]), 0.0)


def body(deflation, layers, layer_table, forcing):
    nx = lax.axis_size("gx")
    ny = lax.axis_size("gy")
    vmem = pl.BlockSpec(memory_space=pltpu.VMEM)
    hbm = pl.BlockSpec(memory_space=pltpu.HBM)
    dma = pltpu.SemaphoreType.DMA
    stages = sum_stages(nx, ny)
    rows, answer = pl.pallas_call(
        functools.partial(kernel, nx, ny),
        out_shape=(
            jax.ShapeDtypeStruct((9, VEC, VEC), F32),
            jax.ShapeDtypeStruct((1, 1, VEC), F32),
        ),
        in_specs=[hbm, hbm, pl.BlockSpec(memory_space=pltpu.SMEM), hbm],
        out_specs=(vmem, vmem),
        scratch_shapes=[
            pltpu.VMEM((EX, EY, VEC, CZ), F32),
            pltpu.VMEM((CY, CX, CZ), jnp.int32),
            pltpu.VMEM((CY, CX, CZ), F32),
            pltpu.VMEM((12, 7, 2, CZ), F32),
            pltpu.VMEM((12, 7, VEC, CZ), F32),
            pltpu.VMEM((12, 7, VEC, CZ), F32),
            pltpu.VMEM((12, 7, 1, CZ), F32),
            pltpu.VMEM((3, EY, VEC, CZ), F32),
            pltpu.VMEM((6, 3, VEC, CZ), F32),
            pltpu.VMEM((len(DOWN), VEC, CZ), F32),
            pltpu.VMEM((3, 3, VEC, CZ), F32),
            pltpu.VMEM((3, 3, VEC, CZ), F32),
            pltpu.VMEM((5, 8, CZ), F32),
            pltpu.VMEM((5, 8, CZ), F32),
            pltpu.VMEM((ITERS, EX, EY, 1, CZ), F32),
            pltpu.VMEM((ITERS, 8, EX, EY, 1, CZ), F32),
            pltpu.VMEM((12, 7, 1, CZ), F32),
            pltpu.VMEM((12, 7, 1, CZ), F32),
            pltpu.VMEM((len(stages), 2, CZ), F32),
            dma((3,)), dma((8,)), dma((8,)), dma((16,)), dma((16,)), dma, dma,
            dma((14,)), dma((14,)), dma((6,)), dma((6,)), dma((5,)), dma((5,)),
            dma((ITERS, 8)), dma((ITERS, 8)), dma((len(stages),)), dma((len(stages),)),
            *[pltpu.VMEM((members(digits) - 1, 2, CZ), F32) for digits in stages],
        ],
        compiler_params=pltpu.CompilerParams(
            collective_id=0, has_side_effects=True, vmem_limit_bytes=32 * 1024 * 1024
        ),
        name="coarse",
    )(
        jnp.transpose(deflation, (1, 2, 0, 3)),
        jnp.transpose(layers, (1, 0, 2)),
        layer_table,
        jnp.transpose(forcing, (1, 0, 2)),
    )
    return rows[None, None], answer


def solution(mesh):
    return jax.shard_map(
        body,
        mesh=mesh,
        in_specs=(P(None, "gx", "gy", None), P("gx", "gy", None), P(), P("gx", "gy", None)),
        out_specs=(P("gx", "gy", None, None, None), P("gx", "gy", None)),
        check_vma=False,
    )
```

```python
import functools
import math

import jax
import jax.numpy as jnp
from jax import lax
from jax.experimental import pallas as pl
from jax.experimental.pallas import tpu as pltpu
from jax.sharding import PartitionSpec as P

VEC = 32
CX = 8
CY = 3
CZ = 128
MARGIN = 1
LAYERS = 85
ITERS = 3
EX = 10
EY = 5
MESH = pl.DeviceIdType.MESH
F32 = jnp.float32
BF16 = jnp.bfloat16

EDGE = (0, 1, 2, 7, 8, 9)
DIRS = ((0, 1), (0, -1), (1, 1), (-1, 1), (1, -1), (-1, -1), (1, 0), (-1, 0))
UP = tuple((n, r) for n in (0, 5, 1, 4) for r in range(3)) + ((2, 0), (2, 1), (3, 0), (3, 1))
DOWN = tuple((c, r) for c in (3, 4, 5, 6) for r in range(3)) + ((2, 2), (7, 2))
UP_SHARE = (0, 4, 4, 4, 4)
DOWN_SHARE = (0, 4, 3, 3, 4)
SEND_X = {1: (8, 2), -1: (2, 2), 0: (2, 8)}
LAND_X = {1: (0, 2), -1: (10, 2), 0: (2, 8)}
SEND_Y = {1: (3, 2), -1: (2, 2), 0: (2, 3)}
LAND_Y = {1: (0, 2), -1: (5, 2), 0: (2, 3)}


HALO_X = {1: (7, 3, 0), -1: (0, 3, 9), 0: (0, 10, 1)}
HALO_Y = {1: (2, 3, 0), -1: (0, 3, 4), 0: (0, 5, 1)}
PAIRS = ((0, 0), (0, 1), (0, 2), (0, 3), (1, 1), (1, 2), (1, 3), (2, 2), (2, 3))
SHRINK = 0.125
QUIET = 1e-13


def sum_stages(nx, ny):
    low_x = 8 if nx % 8 == 0 else 2
    low_y = 4 if ny % 4 == 0 and ny > 4 else 2
    return (
        ((0, 1, low_x),),
        ((0, low_x, nx // low_x), (1, 1, low_y)),
        ((1, low_y, ny // low_y),),
    )


def members(digits):
    return math.prod(count for axis, stride, count in digits)


def two_sum(a, b):
    total = a + b
    back = total - a
    return total, (a - (total - back)) + (b - back)


def quick_sum(a, b):
    total = a + b
    return total, b - (total - a)


def halves(a):
    big = 4097.0 * a
    high = big - (big - a)
    return high, a - high


def two_product(a, b):
    product = a * b
    ah, al = halves(a)
    bh, bl = halves(b)
    return product, ((ah * bh - product) + ah * bl + al * bh) + al * bl


def add2(a, b):
    total, err = two_sum(a[0], b[0])
    return quick_sum(total, err + (a[1] + b[1]))


def mul2(a, b):
    product, err = two_product(a[0], b[0])
    return quick_sum(product, err + (a[0] * b[1] + a[1] * b[0]))


def neg2(a):
    return -a[0], -a[1]


def div2(a, b):
    first = a[0] / b[0]
    rest = add2(a, neg2(mul2(b, (first, jnp.zeros_like(first)))))
    return quick_sum(first, rest[0] / b[0])


def total2(terms):
    result = terms[0]
    for term in terms[1:]:
        result = add2(result, term)
    return result


def three_steps(gram):
    at = {}
    for (i, j), value in zip(PAIRS, gram):
        at[i, j] = at[j, i] = value
    one = (jnp.ones_like(gram[0][0]), jnp.zeros_like(gram[0][0]))
    residual, direction = [one], [one]
    solution = []
    norm = first = at[0, 0]
    for step in range(ITERS):
        size = len(direction)
        energy = total2(
            [
                mul2(mul2(direction[i], direction[j]), at[i, j + 1])
                for i in range(size)
                for j in range(size)
            ]
        )
        length = div2(norm, energy)
        if step > 0:
            live = norm[0] > QUIET * first[0]
            length = tuple(jnp.where(live, part, 0.0) for part in length)
        moved = [mul2(length, d) for d in direction]
        solution = [add2(x, m) for x, m in zip(solution, moved)] + moved[len(solution) :]
        if step == ITERS - 1:
            break
        back = [neg2(m) for m in moved]
        residual = [residual[0]] + [
            add2(residual[k], back[k - 1]) if k < len(residual) else back[k - 1]
            for k in range(1, size + 1)
        ]
        count = len(residual)
        terms = []
        for i in range(count):
            for j in range(i, count):
                term = mul2(mul2(residual[i], residual[j]), at[i, j])
                terms.append(term if i == j else (2.0 * term[0], 2.0 * term[1]))
        norm_next = total2(terms)
        ratio = div2(norm_next, norm)
        if step > 0:
            ratio = tuple(jnp.where(live, part, 0.0) for part in ratio)
        direction = [
            add2(residual[k], mul2(ratio, direction[k])) if k < size else residual[k]
            for k in range(count)
        ]
        norm = norm_next
    return [x[0] for x in solution]


def pack(cells):
    highs = [c.astype(BF16) for c in cells]
    lows = [(c - h.astype(F32)).astype(BF16) for c, h in zip(cells, highs)]
    high = jnp.concatenate(highs, axis=1)
    low = jnp.concatenate(lows, axis=1)
    return jnp.concatenate([high, low], axis=0)


def dot_cells(left, right):
    return lax.dot_general(
        pack(left), pack(right), (((1,), (1,)), ((), ())), preferred_element_type=F32
    )


def fold(wide):
    tall = wide[0:VEC] + wide[VEC:]
    return tall[:, 0:VEC] + tall[:, VEC:]


def squeeze_block(block):
    return jnp.concatenate([block[8 * g : 8 * g + 8] for g in range(4)], axis=1)


def spread_block(packed):
    return jnp.concatenate([packed[:, VEC * g : VEC * g + VEC] for g in range(4)], axis=0)


def kernel(
    nx, ny, raw_hbm, layers_hbm, table, forcing_hbm, rows, answer,
    basis, entry_in, force_in, field, weighted, image, diag, strip_x, strip_y, strip_m,
    corner_r, corner_l, block_out, block_in, spread_out, spread_in, whole, shaded, sum_out,
    l_sem, f_send, f_recv, y_send, y_recv, x_send, x_recv, m_send, m_recv, c_send, c_recv,
    b_send, b_recv, v_send, v_recv, a_send, a_recv, *sums,
):
    px = lax.axis_index("gx")
    py = lax.axis_index("gy")
    stages = sum_stages(nx, ny)
    loads = [
        pltpu.make_async_copy(src, dst, l_sem.at[n])
        for n, (src, dst) in enumerate(
            ((layers_hbm, entry_in), (forcing_hbm, force_in), (raw_hbm, basis))
        )
    ]
    for load_copy in loads:
        load_copy.start()
    right, left = lax.rem(px + 1, nx), lax.rem(px + nx - 1, nx)
    upper, lower = lax.rem(py + 1, ny), lax.rem(py + ny - 1, ny)
    at_x = {1: right, -1: left, 0: px}
    at_y = {1: upper, -1: lower, 0: py}
    has_right, has_left = px < nx - 1, px > 0
    has_up, has_down = py < ny - 1, py > 0

    def remote(src, dst, send, recv, to):
        return pltpu.make_async_remote_copy(
            src_ref=src, dst_ref=dst, send_sem=send, recv_sem=recv, device_id=to, device_id_type=MESH
        )

    barrier = pltpu.get_barrier_semaphore()

    def partner(digits, k):
        place = [px, py]
        for axis, stride, count in digits:
            step, k = k % count, k // count
            digit = lax.rem(lax.div(place[axis], stride), count)
            place[axis] = place[axis] + (lax.rem(digit + step, count) - digit) * stride
        return tuple(place)

    reaches = {1: has_right, -1: has_left}
    hears = {1: has_left, -1: has_right}

    def by_side(act, conditions):
        act(0)
        for side in (1, -1):
            pl.when(conditions[side])(functools.partial(act, side))

    def greet(side):
        for dx, dy in DIRS:
            if dx == side:
                pl.semaphore_signal(
                    barrier, inc=1, device_id=(at_x[dx], at_y[dy]), device_id_type=MESH
                )

    by_side(greet, reaches)

    def start_all(copies):
        def start(side):
            for copy, (dx, dy) in zip(copies, DIRS):
                if dx == side:
                    copy.start()

        by_side(start, reaches)

    def wait_all(copies):
        def sent(side):
            for copy, (dx, dy) in zip(copies, DIRS):
                if dx == side:
                    copy.wait_send()

        def received(side):
            for copy, (dx, dy) in zip(copies, DIRS):
                if dx == side:
                    copy.wait_recv()

        by_side(received, hears)
        by_side(sent, reaches)

    def start_to(side, copy):
        if side == 0:
            copy.start()
        else:
            pl.when(reaches[side])(copy.start)

    def wait_to(side, copy):
        if side == 0:
            copy.wait()
        else:
            pl.when(hears[side])(copy.wait_recv)
            pl.when(reaches[side])(copy.wait_send)
    for digits in stages:
        for k in range(1, members(digits)):
            pl.semaphore_signal(barrier, inc=1, device_id=partner(digits, k), device_id_type=MESH)

    loads[0].wait()
    entry = entry_in[...]

    def look_up(t, root):
        for k in range(5):
            root = jnp.where(entry == 5 * t + k, table[5 * t + k], root)
        return root

    root = jnp.sqrt(lax.fori_loop(0, LAYERS // 5, look_up, jnp.zeros((CY, CX, CZ), F32)))
    loads[1].wait()
    for x in range(CX):
        for y in range(CY):
            field[2 + x, 2 + y, 0:1, :] = root[y, x : x + 1, :]
            field[2 + x, 2 + y, 1:2, :] = force_in[y, x : x + 1, :]

    def weights_of(cells, has_below, has_above):
        low, high = jnp.where(has_below, 0.5, 1.0), jnp.where(has_above, 0.5, 1.0)
        low_end, high_end = jnp.where(has_below, 0.5, 0.0), jnp.where(has_above, 0.5, 0.0)
        return [low_end, low] + [1.0] * (cells - 4) + [high, high_end]

    scale_x = [w * (1.0 / math.sqrt(CX * CY * CZ)) for w in weights_of(EX, has_left, has_right)]
    scale_y = weights_of(EY, has_down, has_up)
    loads[2].wait()
    for ex in range(EX):
        for ey in range(EY):
            basis[ex, ey] = basis[ex, ey] * (scale_x[ex] * scale_y[ey])

    sides = 1 - (px + 1) // nx + (px + nx - 1) // nx
    pl.semaphore_wait(barrier, 2 + 3 * sides + sum(members(d) - 1 for d in stages))

    field_copies = []
    for n, (dx, dy) in enumerate(DIRS):
        sx, lx = SEND_X[dx]
        sy, ly = SEND_Y[dy]
        tx = LAND_X[dx][0]
        ty = LAND_Y[dy][0]
        field_copies.append(
            remote(
                field.at[pl.ds(sx, lx), pl.ds(sy, ly)],
                field.at[pl.ds(tx, lx), pl.ds(ty, ly)],
                f_send.at[n], f_recv.at[n], (at_x[dx], at_y[dy]),
            )
        )
    start_all(field_copies)
    up_copies = [
        remote(basis.at[EDGE[n], r], strip_y.at[n, r], y_send.at[t], y_recv.at[t], (px, lower))
        for t, (n, r) in enumerate(UP)
    ]
    down_copies = [
        remote(image.at[c + 1, 4 + r], strip_m.at[t], m_send.at[t], m_recv.at[t], (px, upper))
        for t, (c, r) in enumerate(DOWN)
    ]

    def feed(gap):
        ups = up_copies[sum(UP_SHARE[:gap]) : sum(UP_SHARE[: gap + 1])]
        downs = down_copies[sum(DOWN_SHARE[:gap]) : sum(DOWN_SHARE[: gap + 1])]
        for t in range(max(len(ups), len(downs))):
            for copies in (ups, downs):
                if t < len(copies):
                    copies[t].start()

    feed(0)
    x_copy = remote(basis.at[pl.ds(0, 3)], strip_x, x_send, x_recv, (left, py))
    start_to(-1, x_copy)

    empty = jnp.zeros((VEC, CZ), F32)
    for j in range(7):
        weighted[0, j] = empty
        weighted[11, j] = empty

    def zero_rows(i, carry):
        weighted[i, 0] = empty
        weighted[i, 6] = empty
        return carry

    lax.fori_loop(1, 11, zero_rows, 0)

    wait_all(field_copies)

    @pl.when(px == 0)
    def _():
        field[0:2] = jnp.zeros((2, 7, 2, CZ), F32)

    @pl.when(px == nx - 1)
    def _():
        field[10:12] = jnp.zeros((2, 7, 2, CZ), F32)

    @pl.when(py == 0)
    def _():
        field[:, 0:2] = jnp.zeros((12, 2, 2, CZ), F32)

    @pl.when(py == ny - 1)
    def _():
        field[:, 5:7] = jnp.zeros((12, 2, 2, CZ), F32)

    lane1 = lax.broadcasted_iota(jnp.int32, (1, CZ), 1)
    lane32 = lax.broadcasted_iota(jnp.int32, (VEC, CZ), 1)

    def beside(value, lane):
        before = jnp.where(lane > 0, pltpu.roll(value, 1, 1), 0.0)
        after = jnp.where(lane < CZ - 1, pltpu.roll(value, CZ - 1, 1), 0.0)
        return before + after

    def scale(i, load):
        for j in range(1, 6):
            value = basis[i - 1, j - 1]
            own = field[i, j, 0:1, :]
            weighted[i, j] = own * value
            load = load + field[i, j, 1:2, :] * value
            near = (
                field[i - 1, j, 0:1, :] + field[i + 1, j, 0:1, :]
                + field[i, j - 1, 0:1, :] + field[i, j + 1, 0:1, :] + beside(own, lane1)
            )
            diag[i, j] = 0.5 + own * near
        return load

    load = lax.fori_loop(1, 11, scale, empty, unroll=5)

    row_id = lax.broadcasted_iota(jnp.int32, (VEC, VEC), 0)
    col_id = lax.broadcasted_iota(jnp.int32, (VEC, VEC), 1)
    diagonal = row_id == col_id

    def as_row(column):
        return jnp.sum(jnp.where(diagonal, column, 0.0), axis=0, keepdims=True)

    def halo_copies(step):
        result = []
        for n, (dx, dy) in enumerate(DIRS):
            sx, lx, unused = HALO_X[dx]
            sy, ly, unused = HALO_Y[dy]
            result.append(
                remote(
                    spread_out.at[step, pl.ds(sx, lx), pl.ds(sy, ly)],
                    spread_in.at[step, n, pl.ds(0, lx), pl.ds(0, ly)],
                    v_send.at[step, n], v_recv.at[step, n], (at_x[dx], at_y[dy]),
                )
            )
        return result

    halos = [halo_copies(step) for step in range(ITERS)]

    def send_spread(step, column):
        def spread(ex, carry):
            for ey in range(EY):
                spread_out[step, ex, ey] = jnp.sum(basis[ex, ey] * column, axis=0, keepdims=True)
            return carry

        lax.fori_loop(0, EX, spread, 0, unroll=True)
        start_all(halos[step])

    exists = {(1, 0): has_left, (-1, 0): has_right, (0, 1): has_down, (0, -1): has_up}

    def gather_back(step):
        whole[...] = jnp.zeros((12, 7, 1, CZ), F32)
        whole[1:11, 1:6] = spread_out[step]
        wait_all(halos[step])
        for n, (dx, dy) in enumerate(DIRS):
            lx, tx = HALO_X[dx][1:]
            ly, ty = HALO_Y[dy][1:]
            there = exists[dx, 0] if dy == 0 else exists[0, dy] if dx == 0 else exists[dx, 0] & exists[0, dy]
            piece = jnp.where(there, spread_in[step, n, 0:lx, 0:ly], 0.0)
            whole[tx : tx + lx, ty : ty + ly] = whole[tx : tx + lx, ty : ty + ly] + piece

        def shade(i, carry):
            for j in range(7):
                shaded[i, j] = field[i, j, 0:1, :] * whole[i, j]
            return carry

        lax.fori_loop(0, 12, shade, 0, unroll=True)

        def collect(i, total):
            for j in range(1, 6):
                near = (
                    shaded[i - 1, j] + shaded[i + 1, j] + shaded[i, j - 1] + shaded[i, j + 1]
                    + beside(shaded[i, j], lane1)
                )
                value = diag[i, j] * whole[i, j] - field[i, j, 0:1, :] * near
                total = total + basis[i - 1, j - 1] * value
            return total

        return jnp.sum(lax.fori_loop(1, 11, collect, empty, unroll=True), axis=1, keepdims=True) * SHRINK

    columns = [jnp.sum(load, axis=1, keepdims=True)]
    send_spread(0, columns[0])

    def image_inside(i, j):
        total = (
            weighted[i - 1, j] + weighted[i + 1, j] + weighted[i, j - 1] + weighted[i, j + 1]
            + beside(weighted[i, j], lane32)
        )
        image[i, j] = diag[i, j] * basis[i - 1, j - 1] - field[i, j, 0:1, :] * total

    def image_above(i):
        image[i, 6] = -(field[i, 6, 0:1, :] * weighted[i, 5])

    def upper_rows(i, carry):
        image_inside(i, 4)
        image_inside(i, 5)
        image_above(i)
        return carry

    def lower_rows(i, carry):
        for j in (1, 2, 3):
            image_inside(i, j)
        return carry

    lax.fori_loop(4, 8, upper_rows, 0)
    lax.fori_loop(1, 4, upper_rows, 0)
    lax.fori_loop(8, 11, upper_rows, 0)
    lax.fori_loop(1, 11, lower_rows, 0)
    for j in (4, 5):
        image[0, j] = -(field[0, j, 0:1, :] * weighted[1, j])
    for j in range(1, 6):
        image[11, j] = -(field[11, j, 0:1, :] * weighted[10, j])
    feed(1)
    two, rest = pl.ds(0, 2), pl.ds(4, 2)
    tall = pl.ds(4, 3)
    corner_copies = [
        (side, remote(src, dst, c_send.at[n], c_recv.at[n], (to, py)))
        for n, (side, src, dst, to) in enumerate(
            (
                (1, image.at[pl.ds(9, 2), tall], corner_r.at[two], right),
                (1, image.at[11, rest], corner_r.at[2, two], right),
                (-1, image.at[pl.ds(1, 2), tall], corner_l.at[pl.ds(1, 2)], left),
                (-1, image.at[0, rest], corner_l.at[0, two], left),
            )
        )
    ]
    for side, copy in corner_copies:
        start_to(side, copy)

    columns.append(gather_back(0))
    send_spread(1, columns[1])

    def own_block(t, total):
        i = 1 + 2 * t
        cells = [(i + k, j) for k in (0, 1) for j in range(1, 6)]
        return total + dot_cells(
            [image[a, b] for a, b in cells], [basis[a - 1, b - 1] for a, b in cells]
        )

    rows[4] = fold(lax.fori_loop(0, 5, own_block, jnp.zeros((2 * VEC, 2 * VEC), F32)))
    feed(2)

    def send_block(n, block, to, side=0):
        block_out[n] = squeeze_block(block)
        copy = remote(block_out.at[n], block_in.at[n], b_send.at[n], b_recv.at[n], to)
        start_to(side, copy)
        return side, copy

    columns.append(gather_back(1))
    send_spread(2, columns[2])

    wait_to(-1, x_copy)
    block_x = fold(
        dot_cells(
            [image[9 + k, 1 + j] for k in range(3) for j in range(EY)],
            [strip_x[k, j] for k in range(3) for j in range(EY)],
        )
    )
    rows[7] = jnp.where(has_right, block_x, 0.0)
    block_copies = [send_block(0, block_x.T, (right, py), 1)]
    feed(3)

    columns.append(gather_back(2))

    blank = jnp.zeros((1, CZ - VEC), F32)
    vectors = [jnp.concatenate([as_row(c), blank], axis=1) for c in columns]
    slot = lax.broadcasted_iota(jnp.int32, (16, CZ), 0)
    lane16 = lax.broadcasted_iota(jnp.int32, (16, CZ), 1)
    one_side = other_side = jnp.zeros((16, CZ), F32)
    for n, (i, j) in enumerate(PAIRS):
        one_side = jnp.where(slot == n, vectors[i], one_side)
        other_side = jnp.where(slot == n, vectors[j], other_side)
    gram = two_product(one_side, other_side)
    for shift in (16, 8, 4, 2, 1):
        gram = add2(gram, tuple(pltpu.roll(part, CZ - shift, 1) for part in gram))
    value = tuple(
        jnp.sum(jnp.where(slot == lane16, part[:, 0:1], 0.0), axis=0, keepdims=True)
        for part in gram
    )

    sum_copies = []

    def tell(stage):
        sum_out[stage] = jnp.concatenate(value, axis=0)
        for k in range(1, members(stages[stage])):
            remote(
                sum_out.at[stage], sums[stage].at[k - 1],
                a_send.at[stage], a_recv.at[stage], partner(stages[stage], k),
            ).start()

    def hear(stage):
        whole_inbox = remote(
            sums[stage], sums[stage], a_send.at[stage], a_recv.at[stage], (right, upper)
        )
        whole_inbox.wait()
        result = value
        for k in range(1, members(stages[stage])):
            message = sums[stage][k - 1]
            result = add2(result, (message[0:1], message[1:2]))
        return result

    tell(0)
    feed(4)
    value = hear(0)
    tell(1)
    for copy in down_copies:
        copy.wait()
    part_m = fold(
        dot_cells([strip_m[t] for t in range(len(DOWN))], [basis[c, r] for c, r in DOWN])
    )
    block_copies.append(send_block(1, part_m, (px, lower)))
    for copy in up_copies:
        copy.wait()
    part_e = fold(
        dot_cells(
            [image[EDGE[n] + 1, 4 + r] for n, r in UP], [strip_y[n, r] for n, r in UP]
        )
    )
    block_copies.append(send_block(2, part_e.T, (px, upper)))
    for side, copy in corner_copies:
        wait_to(side, copy)
    block_l = fold(
        dot_cells(
            [corner_r[n, r] for n, r in UP if n < 3], [strip_y[n, r] for n, r in UP if n < 3]
        )
    )
    block_copies.append(send_block(3, block_l.T, (px, upper)))
    block_copies.append(send_block(5, block_l, (left, py), -1))
    block_r = fold(
        dot_cells(
            [corner_l[n - 3, r] for n, r in UP if n > 2], [strip_y[n, r] for n, r in UP if n > 2]
        )
    )
    block_copies.append(send_block(4, block_r.T, (px, upper)))
    block_copies.append(send_block(6, block_r, (right, py), 1))
    value = hear(1)
    tell(2)
    value = hear(2)
    steps = three_steps([tuple(part[:, n : n + 1] for part in value) for n in range(len(PAIRS))])
    found = SHRINK * (steps[0] * vectors[0] + steps[1] * vectors[1] + steps[2] * vectors[2])
    answer[0] = found[:, 0:VEC]

    for side, copy in block_copies:
        wait_to(side, copy)
    rows[1] = jnp.where(has_left, spread_block(block_in[0]), 0.0)
    rows[5] = jnp.where(has_up, part_e + spread_block(block_in[1]), 0.0)
    rows[3] = jnp.where(has_down, part_m.T + spread_block(block_in[2]), 0.0)
    rows[0] = jnp.where(has_left & has_down, spread_block(block_in[3]), 0.0)
    rows[8] = jnp.where(has_right & has_up, spread_block(block_in[5]), 0.0)
    rows[2] = jnp.where(has_left & has_up, spread_block(block_in[6]), 0.0)
    rows[6] = jnp.where(has_right & has_down, spread_block(block_in[4]), 0.0)


def body(deflation, layers, layer_table, forcing):
    nx = lax.axis_size("gx")
    ny = lax.axis_size("gy")
    vmem = pl.BlockSpec(memory_space=pltpu.VMEM)
    hbm = pl.BlockSpec(memory_space=pltpu.HBM)
    dma = pltpu.SemaphoreType.DMA
    stages = sum_stages(nx, ny)
    rows, answer = pl.pallas_call(
        functools.partial(kernel, nx, ny),
        out_shape=(
            jax.ShapeDtypeStruct((9, VEC, VEC), F32),
            jax.ShapeDtypeStruct((1, 1, VEC), F32),
        ),
        in_specs=[hbm, hbm, pl.BlockSpec(memory_space=pltpu.SMEM), hbm],
        out_specs=(vmem, vmem),
        scratch_shapes=[
            pltpu.VMEM((EX, EY, VEC, CZ), F32),
            pltpu.VMEM((CY, CX, CZ), jnp.int32),
            pltpu.VMEM((CY, CX, CZ), F32),
            pltpu.VMEM((12, 7, 2, CZ), F32),
            pltpu.VMEM((12, 7, VEC, CZ), F32),
            pltpu.VMEM((12, 7, VEC, CZ), F32),
            pltpu.VMEM((12, 7, 1, CZ), F32),
            pltpu.VMEM((3, EY, VEC, CZ), F32),
            pltpu.VMEM((6, 3, VEC, CZ), F32),
            pltpu.VMEM((len(DOWN), VEC, CZ), F32),
            pltpu.VMEM((3, 3, VEC, CZ), F32),
            pltpu.VMEM((3, 3, VEC, CZ), F32),
            pltpu.VMEM((7, 8, CZ), F32),
            pltpu.VMEM((7, 8, CZ), F32),
            pltpu.VMEM((ITERS, EX, EY, 1, CZ), F32),
            pltpu.VMEM((ITERS, 8, EX, EY, 1, CZ), F32),
            pltpu.VMEM((12, 7, 1, CZ), F32),
            pltpu.VMEM((12, 7, 1, CZ), F32),
            pltpu.VMEM((len(stages), 2, CZ), F32),
            dma((3,)), dma((8,)), dma((8,)), dma((16,)), dma((16,)), dma, dma,
            dma((14,)), dma((14,)), dma((4,)), dma((4,)), dma((7,)), dma((7,)),
            dma((ITERS, 8)), dma((ITERS, 8)), dma((len(stages),)), dma((len(stages),)),
            *[pltpu.VMEM((members(digits) - 1, 2, CZ), F32) for digits in stages],
        ],
        compiler_params=pltpu.CompilerParams(
            collective_id=0, has_side_effects=True, vmem_limit_bytes=32 * 1024 * 1024
        ),
        name="coarse",
    )(
        jnp.transpose(deflation, (1, 2, 0, 3)),
        jnp.transpose(layers, (1, 0, 2)),
        layer_table,
        jnp.transpose(forcing, (1, 0, 2)),
    )
    return rows[None, None], answer


def solution(mesh):
    return jax.shard_map(
        body,
        mesh=mesh,
        in_specs=(P(None, "gx", "gy", None), P("gx", "gy", None), P(), P("gx", "gy", None)),
        out_specs=(P("gx", "gy", None, None, None), P("gx", "gy", None)),
        check_vma=False,
    )
```

```python
import functools
import math

import jax
import jax.numpy as jnp
from jax import lax
from jax.experimental import pallas as pl
from jax.experimental.pallas import tpu as pltpu
from jax.sharding import PartitionSpec as P

VEC = 32
CX = 8
CY = 3
CZ = 128
MARGIN = 1
LAYERS = 85
ITERS = 3
EX = 10
EY = 5
MESH = pl.DeviceIdType.MESH
F32 = jnp.float32
BF16 = jnp.bfloat16

EDGE = (0, 1, 2, 7, 8, 9)
DIRS = ((0, 1), (0, -1), (1, 1), (-1, 1), (1, -1), (-1, -1), (1, 0), (-1, 0))
UP = tuple((n, r) for n in (0, 5, 1, 4) for r in range(3)) + ((2, 0), (2, 1), (3, 0), (3, 1))
DOWN = tuple((c, r) for c in (3, 4, 5, 6) for r in range(3)) + ((2, 2), (7, 2))
UP_SHARE = (0, 4, 4, 4, 4)
DOWN_SHARE = (0, 4, 3, 3, 4)
SEND_X = {1: (8, 2), -1: (2, 2), 0: (2, 8)}
LAND_X = {1: (0, 2), -1: (10, 2), 0: (2, 8)}
SEND_Y = {1: (3, 2), -1: (2, 2), 0: (2, 3)}
LAND_Y = {1: (0, 2), -1: (5, 2), 0: (2, 3)}


HALO_X = {1: (7, 3, 0), -1: (0, 3, 9), 0: (0, 10, 1)}
HALO_Y = {1: (2, 3, 0), -1: (0, 3, 4), 0: (0, 5, 1)}
PAIRS = ((0, 0), (0, 1), (0, 2), (0, 3), (1, 1), (1, 2), (1, 3), (2, 2), (2, 3))
SHRINK = 0.125
QUIET = 1e-13


def sum_stages(nx, ny):
    low_x = 8 if nx % 8 == 0 else 2
    low_y = 4 if ny % 4 == 0 and ny > 4 else 2
    return (
        ((0, 1, low_x),),
        ((0, low_x, nx // low_x), (1, 1, low_y)),
        ((1, low_y, ny // low_y),),
    )


def members(digits):
    return math.prod(count for axis, stride, count in digits)


def two_sum(a, b):
    total = a + b
    back = total - a
    return total, (a - (total - back)) + (b - back)


def quick_sum(a, b):
    total = a + b
    return total, b - (total - a)


def halves(a):
    big = 4097.0 * a
    high = big - (big - a)
    return high, a - high


def two_product(a, b):
    product = a * b
    ah, al = halves(a)
    bh, bl = halves(b)
    return product, ((ah * bh - product) + ah * bl + al * bh) + al * bl


def add2(a, b):
    total, err = two_sum(a[0], b[0])
    return quick_sum(total, err + (a[1] + b[1]))


def mul2(a, b):
    product, err = two_product(a[0], b[0])
    return quick_sum(product, err + (a[0] * b[1] + a[1] * b[0]))


def neg2(a):
    return -a[0], -a[1]


def div2(a, b):
    first = a[0] / b[0]
    rest = add2(a, neg2(mul2(b, (first, jnp.zeros_like(first)))))
    return quick_sum(first, rest[0] / b[0])


def total2(terms):
    result = terms[0]
    for term in terms[1:]:
        result = add2(result, term)
    return result


def three_steps(gram):
    at = {}
    for (i, j), value in zip(PAIRS, gram):
        at[i, j] = at[j, i] = value
    one = (jnp.ones_like(gram[0][0]), jnp.zeros_like(gram[0][0]))
    residual, direction = [one], [one]
    solution = []
    norm = first = at[0, 0]
    for step in range(ITERS):
        size = len(direction)
        energy = total2(
            [
                mul2(mul2(direction[i], direction[j]), at[i, j + 1])
                for i in range(size)
                for j in range(size)
            ]
        )
        length = div2(norm, energy)
        if step > 0:
            live = norm[0] > QUIET * first[0]
            length = tuple(jnp.where(live, part, 0.0) for part in length)
        moved = [mul2(length, d) for d in direction]
        solution = [add2(x, m) for x, m in zip(solution, moved)] + moved[len(solution) :]
        if step == ITERS - 1:
            break
        back = [neg2(m) for m in moved]
        residual = [residual[0]] + [
            add2(residual[k], back[k - 1]) if k < len(residual) else back[k - 1]
            for k in range(1, size + 1)
        ]
        count = len(residual)
        terms = []
        for i in range(count):
            for j in range(i, count):
                term = mul2(mul2(residual[i], residual[j]), at[i, j])
                terms.append(term if i == j else (2.0 * term[0], 2.0 * term[1]))
        norm_next = total2(terms)
        ratio = div2(norm_next, norm)
        if step > 0:
            ratio = tuple(jnp.where(live, part, 0.0) for part in ratio)
        direction = [
            add2(residual[k], mul2(ratio, direction[k])) if k < size else residual[k]
            for k in range(count)
        ]
        norm = norm_next
    return [x[0] for x in solution]


def pack(cells):
    highs = [c.astype(BF16) for c in cells]
    lows = [(c - h.astype(F32)).astype(BF16) for c, h in zip(cells, highs)]
    high = jnp.concatenate(highs, axis=1)
    low = jnp.concatenate(lows, axis=1)
    return jnp.concatenate([high, low], axis=0)


def dot_cells(left, right):
    return lax.dot_general(
        pack(left), pack(right), (((1,), (1,)), ((), ())), preferred_element_type=F32
    )


def fold(wide):
    tall = wide[0:VEC] + wide[VEC:]
    return tall[:, 0:VEC] + tall[:, VEC:]


def squeeze_block(block):
    return jnp.concatenate([block[8 * g : 8 * g + 8] for g in range(4)], axis=1)


def spread_block(packed):
    return jnp.concatenate([packed[:, VEC * g : VEC * g + VEC] for g in range(4)], axis=0)


def kernel(
    nx, ny, raw_hbm, layers_hbm, table, forcing_hbm, rows, answer,
    basis, entry_in, force_in, field, weighted, image, diag, strip_x, strip_y, strip_m,
    corner_r, corner_l, block_out, block_in, spread_out, spread_in, whole, shaded, sum_out,
    l_sem, f_send, f_recv, y_send, y_recv, x_send, x_recv, m_send, m_recv, c_send, c_recv,
    b_send, b_recv, v_send, v_recv, a_send, a_recv, *sums,
):
    px = lax.axis_index("gx")
    py = lax.axis_index("gy")
    stages = sum_stages(nx, ny)
    loads = [
        pltpu.make_async_copy(src, dst, l_sem.at[n])
        for n, (src, dst) in enumerate(
            ((layers_hbm, entry_in), (forcing_hbm, force_in), (raw_hbm, basis))
        )
    ]
    for load_copy in loads:
        load_copy.start()
    right, left = lax.rem(px + 1, nx), lax.rem(px + nx - 1, nx)
    upper, lower = lax.rem(py + 1, ny), lax.rem(py + ny - 1, ny)
    at_x = {1: right, -1: left, 0: px}
    at_y = {1: upper, -1: lower, 0: py}
    has_right, has_left = px < nx - 1, px > 0
    has_up, has_down = py < ny - 1, py > 0

    def remote(src, dst, send, recv, to):
        return pltpu.make_async_remote_copy(
            src_ref=src, dst_ref=dst, send_sem=send, recv_sem=recv, device_id=to, device_id_type=MESH
        )

    barrier = pltpu.get_barrier_semaphore()

    def partner(digits, k):
        place = [px, py]
        for axis, stride, count in digits:
            step, k = k % count, k // count
            digit = lax.rem(lax.div(place[axis], stride), count)
            place[axis] = place[axis] + (lax.rem(digit + step, count) - digit) * stride
        return tuple(place)

    reaches = {1: has_right, -1: has_left}
    hears = {1: has_left, -1: has_right}

    def by_side(act, conditions):
        act(0)
        for side in (1, -1):
            pl.when(conditions[side])(functools.partial(act, side))

    def greet(side):
        for dx, dy in DIRS:
            if dx == side:
                pl.semaphore_signal(
                    barrier, inc=1, device_id=(at_x[dx], at_y[dy]), device_id_type=MESH
                )

    by_side(greet, reaches)

    def start_all(copies):
        def start(side):
            for copy, (dx, dy) in zip(copies, DIRS):
                if dx == side:
                    copy.start()

        by_side(start, reaches)

    def wait_all(copies):
        def sent(side):
            for copy, (dx, dy) in zip(copies, DIRS):
                if dx == side:
                    copy.wait_send()

        def received(side):
            for copy, (dx, dy) in zip(copies, DIRS):
                if dx == side:
                    copy.wait_recv()

        by_side(received, hears)
        by_side(sent, reaches)

    def start_to(side, copy):
        if side == 0:
            copy.start()
        else:
            pl.when(reaches[side])(copy.start)

    def wait_to(side, copy):
        if side == 0:
            copy.wait()
        else:
            pl.when(hears[side])(copy.wait_recv)
            pl.when(reaches[side])(copy.wait_send)
    for digits in stages:
        for k in range(1, members(digits)):
            pl.semaphore_signal(barrier, inc=1, device_id=partner(digits, k), device_id_type=MESH)

    loads[0].wait()
    entry = entry_in[...]

    def look_up(t, root):
        for k in range(5):
            root = jnp.where(entry == 5 * t + k, table[5 * t + k], root)
        return root

    root = jnp.sqrt(lax.fori_loop(0, LAYERS // 5, look_up, jnp.zeros((CY, CX, CZ), F32)))
    loads[1].wait()
    for x in range(CX):
        for y in range(CY):
            field[2 + x, 2 + y, 0:1, :] = root[y, x : x + 1, :]
            field[2 + x, 2 + y, 1:2, :] = force_in[y, x : x + 1, :]

    def weights_of(cells, has_below, has_above):
        low, high = jnp.where(has_below, 0.5, 1.0), jnp.where(has_above, 0.5, 1.0)
        low_end, high_end = jnp.where(has_below, 0.5, 0.0), jnp.where(has_above, 0.5, 0.0)
        return [low_end, low] + [1.0] * (cells - 4) + [high, high_end]

    scale_x = [w * (1.0 / math.sqrt(CX * CY * CZ)) for w in weights_of(EX, has_left, has_right)]
    scale_y = weights_of(EY, has_down, has_up)
    loads[2].wait()
    for ex in range(EX):
        for ey in range(EY):
            basis[ex, ey] = basis[ex, ey] * (scale_x[ex] * scale_y[ey])

    sides = 1 - (px + 1) // nx + (px + nx - 1) // nx
    pl.semaphore_wait(barrier, 2 + 3 * sides + sum(members(d) - 1 for d in stages))

    field_copies = []
    for n, (dx, dy) in enumerate(DIRS):
        sx, lx = SEND_X[dx]
        sy, ly = SEND_Y[dy]
        tx = LAND_X[dx][0]
        ty = LAND_Y[dy][0]
        field_copies.append(
            remote(
                field.at[pl.ds(sx, lx), pl.ds(sy, ly)],
                field.at[pl.ds(tx, lx), pl.ds(ty, ly)],
                f_send.at[n], f_recv.at[n], (at_x[dx], at_y[dy]),
            )
        )
    start_all(field_copies)
    up_copies = [
        remote(basis.at[EDGE[n], r], strip_y.at[n, r], y_send.at[t], y_recv.at[t], (px, lower))
        for t, (n, r) in enumerate(UP)
    ]
    down_copies = [
        remote(image.at[c + 1, 4 + r], strip_m.at[t], m_send.at[t], m_recv.at[t], (px, upper))
        for t, (c, r) in enumerate(DOWN)
    ]

    def feed(gap):
        ups = up_copies[sum(UP_SHARE[:gap]) : sum(UP_SHARE[: gap + 1])]
        downs = down_copies[sum(DOWN_SHARE[:gap]) : sum(DOWN_SHARE[: gap + 1])]
        for t in range(max(len(ups), len(downs))):
            for copies in (ups, downs):
                if t < len(copies):
                    copies[t].start()

    feed(0)
    x_copy = remote(basis.at[pl.ds(0, 3)], strip_x, x_send, x_recv, (left, py))
    start_to(-1, x_copy)

    empty = jnp.zeros((VEC, CZ), F32)
    for j in range(7):
        weighted[0, j] = empty
        weighted[11, j] = empty

    def zero_rows(i, carry):
        weighted[i, 0] = empty
        weighted[i, 6] = empty
        return carry

    lax.fori_loop(1, 11, zero_rows, 0)

    wait_all(field_copies)

    @pl.when(px == 0)
    def _():
        field[0:2] = jnp.zeros((2, 7, 2, CZ), F32)

    @pl.when(px == nx - 1)
    def _():
        field[10:12] = jnp.zeros((2, 7, 2, CZ), F32)

    @pl.when(py == 0)
    def _():
        field[:, 0:2] = jnp.zeros((12, 2, 2, CZ), F32)

    @pl.when(py == ny - 1)
    def _():
        field[:, 5:7] = jnp.zeros((12, 2, 2, CZ), F32)

    lane1 = lax.broadcasted_iota(jnp.int32, (1, CZ), 1)
    lane32 = lax.broadcasted_iota(jnp.int32, (VEC, CZ), 1)

    def beside(value, lane):
        before = jnp.where(lane > 0, pltpu.roll(value, 1, 1), 0.0)
        after = jnp.where(lane < CZ - 1, pltpu.roll(value, CZ - 1, 1), 0.0)
        return before + after

    def scale(i, load):
        for j in range(1, 6):
            value = basis[i - 1, j - 1]
            own = field[i, j, 0:1, :]
            weighted[i, j] = own * value
            load = load + field[i, j, 1:2, :] * value
            near = (
                field[i - 1, j, 0:1, :] + field[i + 1, j, 0:1, :]
                + field[i, j - 1, 0:1, :] + field[i, j + 1, 0:1, :] + beside(own, lane1)
            )
            diag[i, j] = 0.5 + own * near
        return load

    load = lax.fori_loop(1, 11, scale, empty, unroll=5)

    row_id = lax.broadcasted_iota(jnp.int32, (VEC, VEC), 0)
    col_id = lax.broadcasted_iota(jnp.int32, (VEC, VEC), 1)
    diagonal = row_id == col_id

    def as_row(column):
        return jnp.sum(jnp.where(diagonal, column, 0.0), axis=0, keepdims=True)

    def halo_copies(step):
        result = []
        for n, (dx, dy) in enumerate(DIRS):
            sx, lx, unused = HALO_X[dx]
            sy, ly, unused = HALO_Y[dy]
            result.append(
                remote(
                    spread_out.at[step, pl.ds(sx, lx), pl.ds(sy, ly)],
                    spread_in.at[step, n, pl.ds(0, lx), pl.ds(0, ly)],
                    v_send.at[step, n], v_recv.at[step, n], (at_x[dx], at_y[dy]),
                )
            )
        return result

    halos = [halo_copies(step) for step in range(ITERS)]

    def send_spread(step, column):
        def spread(ex, carry):
            for ey in range(EY):
                spread_out[step, ex, ey] = jnp.sum(basis[ex, ey] * column, axis=0, keepdims=True)
            return carry

        lax.fori_loop(0, EX, spread, 0, unroll=True)
        start_all(halos[step])

    exists = {(1, 0): has_left, (-1, 0): has_right, (0, 1): has_down, (0, -1): has_up}

    def gather_back(step):
        whole[...] = jnp.zeros((12, 7, 1, CZ), F32)
        whole[1:11, 1:6] = spread_out[step]
        wait_all(halos[step])
        for n, (dx, dy) in enumerate(DIRS):
            lx, tx = HALO_X[dx][1:]
            ly, ty = HALO_Y[dy][1:]
            there = exists[dx, 0] if dy == 0 else exists[0, dy] if dx == 0 else exists[dx, 0] & exists[0, dy]
            piece = jnp.where(there, spread_in[step, n, 0:lx, 0:ly], 0.0)
            whole[tx : tx + lx, ty : ty + ly] = whole[tx : tx + lx, ty : ty + ly] + piece

        def shade(i, carry):
            for j in range(7):
                shaded[i, j] = field[i, j, 0:1, :] * whole[i, j]
            return carry

        lax.fori_loop(0, 12, shade, 0, unroll=True)

        def collect(i, total):
            for j in range(1, 6):
                near = (
                    shaded[i - 1, j] + shaded[i + 1, j] + shaded[i, j - 1] + shaded[i, j + 1]
                    + beside(shaded[i, j], lane1)
                )
                value = diag[i, j] * whole[i, j] - field[i, j, 0:1, :] * near
                total = total + basis[i - 1, j - 1] * value
            return total

        return jnp.sum(lax.fori_loop(1, 11, collect, empty, unroll=True), axis=1, keepdims=True) * SHRINK

    columns = [jnp.sum(load, axis=1, keepdims=True)]
    send_spread(0, columns[0])

    def image_inside(i, j):
        total = (
            weighted[i - 1, j] + weighted[i + 1, j] + weighted[i, j - 1] + weighted[i, j + 1]
            + beside(weighted[i, j], lane32)
        )
        image[i, j] = diag[i, j] * basis[i - 1, j - 1] - field[i, j, 0:1, :] * total

    def image_above(i):
        image[i, 6] = -(field[i, 6, 0:1, :] * weighted[i, 5])

    def upper_rows(i, carry):
        image_inside(i, 4)
        image_inside(i, 5)
        image_above(i)
        return carry

    def lower_rows(i, carry):
        for j in (1, 2, 3):
            image_inside(i, j)
        return carry

    lax.fori_loop(4, 8, upper_rows, 0)
    lax.fori_loop(1, 4, upper_rows, 0)
    lax.fori_loop(8, 11, upper_rows, 0)
    lax.fori_loop(1, 11, lower_rows, 0)
    for j in (4, 5):
        image[0, j] = -(field[0, j, 0:1, :] * weighted[1, j])
    for j in range(1, 6):
        image[11, j] = -(field[11, j, 0:1, :] * weighted[10, j])
    feed(1)
    two, rest = pl.ds(0, 2), pl.ds(4, 2)
    tall = pl.ds(4, 3)
    corner_copies = [
        (side, remote(src, dst, c_send.at[n], c_recv.at[n], (to, py)))
        for n, (side, src, dst, to) in enumerate(
            (
                (1, image.at[pl.ds(9, 2), tall], corner_r.at[two], right),
                (1, image.at[11, rest], corner_r.at[2, two], right),
                (-1, image.at[pl.ds(1, 2), tall], corner_l.at[pl.ds(1, 2)], left),
                (-1, image.at[0, rest], corner_l.at[0, two], left),
            )
        )
    ]

    columns.append(gather_back(0))
    send_spread(1, columns[1])

    def own_block(t, total):
        i = 1 + 2 * t
        cells = [(i + k, j) for k in (0, 1) for j in range(1, 6)]
        return total + dot_cells(
            [image[a, b] for a, b in cells], [basis[a - 1, b - 1] for a, b in cells]
        )

    rows[4] = fold(lax.fori_loop(0, 5, own_block, jnp.zeros((2 * VEC, 2 * VEC), F32)))
    feed(2)

    def send_block(n, block, to, side=0):
        block_out[n] = squeeze_block(block)
        copy = remote(block_out.at[n], block_in.at[n], b_send.at[n], b_recv.at[n], to)
        start_to(side, copy)
        return side, copy

    columns.append(gather_back(1))
    send_spread(2, columns[2])

    wait_to(-1, x_copy)
    block_x = fold(
        dot_cells(
            [image[9 + k, 1 + j] for k in range(3) for j in range(EY)],
            [strip_x[k, j] for k in range(3) for j in range(EY)],
        )
    )
    rows[7] = jnp.where(has_right, block_x, 0.0)
    block_copies = [send_block(0, block_x.T, (right, py), 1)]
    feed(3)
    for side, copy in corner_copies:
        start_to(side, copy)

    columns.append(gather_back(2))

    blank = jnp.zeros((1, CZ - VEC), F32)
    vectors = [jnp.concatenate([as_row(c), blank], axis=1) for c in columns]
    slot = lax.broadcasted_iota(jnp.int32, (16, CZ), 0)
    lane16 = lax.broadcasted_iota(jnp.int32, (16, CZ), 1)
    one_side = other_side = jnp.zeros((16, CZ), F32)
    for n, (i, j) in enumerate(PAIRS):
        one_side = jnp.where(slot == n, vectors[i], one_side)
        other_side = jnp.where(slot == n, vectors[j], other_side)
    gram = two_product(one_side, other_side)
    for shift in (16, 8, 4, 2, 1):
        gram = add2(gram, tuple(pltpu.roll(part, CZ - shift, 1) for part in gram))
    value = tuple(
        jnp.sum(jnp.where(slot == lane16, part[:, 0:1], 0.0), axis=0, keepdims=True)
        for part in gram
    )

    sum_copies = []

    def tell(stage):
        sum_out[stage] = jnp.concatenate(value, axis=0)
        for k in range(1, members(stages[stage])):
            remote(
                sum_out.at[stage], sums[stage].at[k - 1],
                a_send.at[stage], a_recv.at[stage], partner(stages[stage], k),
            ).start()

    def hear(stage):
        whole_inbox = remote(
            sums[stage], sums[stage], a_send.at[stage], a_recv.at[stage], (right, upper)
        )
        whole_inbox.wait()
        result = value
        for k in range(1, members(stages[stage])):
            message = sums[stage][k - 1]
            result = add2(result, (message[0:1], message[1:2]))
        return result

    tell(0)
    feed(4)
    value = hear(0)
    tell(1)
    for copy in down_copies:
        copy.wait()
    part_m = fold(
        dot_cells([strip_m[t] for t in range(len(DOWN))], [basis[c, r] for c, r in DOWN])
    )
    block_copies.append(send_block(1, part_m, (px, lower)))
    for copy in up_copies:
        copy.wait()
    part_e = fold(
        dot_cells(
            [image[EDGE[n] + 1, 4 + r] for n, r in UP], [strip_y[n, r] for n, r in UP]
        )
    )
    block_copies.append(send_block(2, part_e.T, (px, upper)))
    for side, copy in corner_copies:
        wait_to(side, copy)
    block_l = fold(
        dot_cells(
            [corner_r[n, r] for n, r in UP if n < 3], [strip_y[n, r] for n, r in UP if n < 3]
        )
    )
    block_copies.append(send_block(3, block_l.T, (px, upper)))
    block_copies.append(send_block(5, block_l, (left, py), -1))
    block_r = fold(
        dot_cells(
            [corner_l[n - 3, r] for n, r in UP if n > 2], [strip_y[n, r] for n, r in UP if n > 2]
        )
    )
    block_copies.append(send_block(4, block_r.T, (px, upper)))
    block_copies.append(send_block(6, block_r, (right, py), 1))
    value = hear(1)
    tell(2)
    value = hear(2)
    steps = three_steps([tuple(part[:, n : n + 1] for part in value) for n in range(len(PAIRS))])
    found = SHRINK * (steps[0] * vectors[0] + steps[1] * vectors[1] + steps[2] * vectors[2])
    answer[0] = found[:, 0:VEC]

    for side, copy in block_copies:
        wait_to(side, copy)
    rows[1] = jnp.where(has_left, spread_block(block_in[0]), 0.0)
    rows[5] = jnp.where(has_up, part_e + spread_block(block_in[1]), 0.0)
    rows[3] = jnp.where(has_down, part_m.T + spread_block(block_in[2]), 0.0)
    rows[0] = jnp.where(has_left & has_down, spread_block(block_in[3]), 0.0)
    rows[8] = jnp.where(has_right & has_up, spread_block(block_in[5]), 0.0)
    rows[2] = jnp.where(has_left & has_up, spread_block(block_in[6]), 0.0)
    rows[6] = jnp.where(has_right & has_down, spread_block(block_in[4]), 0.0)


def body(deflation, layers, layer_table, forcing):
    nx = lax.axis_size("gx")
    ny = lax.axis_size("gy")
    vmem = pl.BlockSpec(memory_space=pltpu.VMEM)
    hbm = pl.BlockSpec(memory_space=pltpu.HBM)
    dma = pltpu.SemaphoreType.DMA
    stages = sum_stages(nx, ny)
    rows, answer = pl.pallas_call(
        functools.partial(kernel, nx, ny),
        out_shape=(
            jax.ShapeDtypeStruct((9, VEC, VEC), F32),
            jax.ShapeDtypeStruct((1, 1, VEC), F32),
        ),
        in_specs=[hbm, hbm, pl.BlockSpec(memory_space=pltpu.SMEM), hbm],
        out_specs=(vmem, vmem),
        scratch_shapes=[
            pltpu.VMEM((EX, EY, VEC, CZ), F32),
            pltpu.VMEM((CY, CX, CZ), jnp.int32),
            pltpu.VMEM((CY, CX, CZ), F32),
            pltpu.VMEM((12, 7, 2, CZ), F32),
            pltpu.VMEM((12, 7, VEC, CZ), F32),
            pltpu.VMEM((12, 7, VEC, CZ), F32),
            pltpu.VMEM((12, 7, 1, CZ), F32),
            pltpu.VMEM((3, EY, VEC, CZ), F32),
            pltpu.VMEM((6, 3, VEC, CZ), F32),
            pltpu.VMEM((len(DOWN), VEC, CZ), F32),
            pltpu.VMEM((3, 3, VEC, CZ), F32),
            pltpu.VMEM((3, 3, VEC, CZ), F32),
            pltpu.VMEM((7, 8, CZ), F32),
            pltpu.VMEM((7, 8, CZ), F32),
            pltpu.VMEM((ITERS, EX, EY, 1, CZ), F32),
            pltpu.VMEM((ITERS, 8, EX, EY, 1, CZ), F32),
            pltpu.VMEM((12, 7, 1, CZ), F32),
            pltpu.VMEM((12, 7, 1, CZ), F32),
            pltpu.VMEM((len(stages), 2, CZ), F32),
            dma((3,)), dma((8,)), dma((8,)), dma((16,)), dma((16,)), dma, dma,
            dma((14,)), dma((14,)), dma((4,)), dma((4,)), dma((7,)), dma((7,)),
            dma((ITERS, 8)), dma((ITERS, 8)), dma((len(stages),)), dma((len(stages),)),
            *[pltpu.VMEM((members(digits) - 1, 2, CZ), F32) for digits in stages],
        ],
        compiler_params=pltpu.CompilerParams(
            collective_id=0, has_side_effects=True, vmem_limit_bytes=32 * 1024 * 1024
        ),
        name="coarse",
    )(
        jnp.transpose(deflation, (1, 2, 0, 3)),
        jnp.transpose(layers, (1, 0, 2)),
        layer_table,
        jnp.transpose(forcing, (1, 0, 2)),
    )
    return rows[None, None], answer


def solution(mesh):
    return jax.shard_map(
        body,
        mesh=mesh,
        in_specs=(P(None, "gx", "gy", None), P("gx", "gy", None), P(), P("gx", "gy", None)),
        out_specs=(P("gx", "gy", None, None, None), P("gx", "gy", None)),
        check_vma=False,
    )
```
